256 devices in a mesh: ctx: 32 (over y, x, core), tp: 8 (over z).
Axes of the slice: x: 4, y: 4, z: 8, core: 2. Of those that a mesh axis runs over, the one named last changes fastest.
Arguments:
- tokens: bfloat16 [8192, 8192], P('ctx', 'tp'), may hold values from -6 to 6
- frozen: bfloat16 [8192, 3, 8192], P('ctx', None, 'tp'), may hold values from -3 to 3
- cotangent: bfloat16 [8192, 8192], P('ctx', 'tp'), may hold values from -0.119628906 to 0.119628906
- adapter_down_weight: bfloat16 [16, 8192], P(None, 'tp'), may hold values from -0.0625 to 0.0625
- adapter_up_weight: bfloat16 [16, 3, 8192], P(None, None, 'tp'), may hold values from -0.75 to 0.75
- short_depthwise_filter: bfloat16 [3, 3, 8192], P(None, None, 'tp'), may hold values from -3.5 to 3.5
- long_group_filter: bfloat16 [512, 128], P('tp'), may hold values from -8 to 8
- skip_direct_scale: float32 [8192], P('tp'), may hold values from -3 to 3
- document_lengths: int32 [64], replicated, may hold values from 1 to 1024, 8192 in all
- window_row_position: int32 [8192], P('ctx'), may hold values from 0 to 8191, as said below
Outputs:
- mixer_out: bfloat16 [8192, 8192], P('ctx', 'tp')
- grad_down: float32 [16, 8192], P(None, 'tp')
- up_gradient: float32 [16, 3, 8192], P(None, None, 'tp')
- grad_short: float32 [3, 3, 8192], P(None, None, 'tp')
- grad_long: float32 [512, 128], P('tp')
- grad_skip: float32 [8192], P('tp')
The draws below stay inside these ranges and needn't reach their ends.
Inputs may be any that keep to these rules, and one draw needn't show every extreme that they name: `window_row_position`: a permutation of the window's positions; the rows of one loader device (one index of ctx) go to each context shard (places j * 256 to (j + 1) * 256 - 1) in a count of 0, 8 or 16, and in a count of 16 to at least one shard. `document_lengths`: the documents lie end to end in the window in this order; the lengths sum to 8192.
All inputs are finite; a program needn't handle non-finite values.
Results may differ from the reference program's by a relative error of at most 0.0055.
The reference program's roundings to bfloat16 on the way count: a program that leaves them out, or rounds other values in their place, can miss the bound.
Values may be sent and summed in bfloat16 or wider, within the bound.
No kernel may reach another device: no remote copies, remote signals or barrier semaphores. Data moves between devices by JAX's collectives and lax.ppermute only.
A program may use at most 128 MiB of HBM per device.

```python
import math
import jax
import jax.numpy as jnp
import numpy as np
from jax import lax

MIXER_WIDTH = 8192
ADAPTER_RANK = 16
TAPS = 128
SHORT_TAPS = 3
TOK_DEV = 256
WINDOW = 8192
GROUPS = 512
DOCS = 64
LONGEST = 1024
N_TP = 8


def draw_window_row_position(key, part):
    shards = WINDOW // TOK_DEV
    share_count = TOK_DEV // shards
    key_order, key_place, key_slots = jax.random.split(key, 3)
    shard_ids = jnp.arange(shards, dtype=jnp.int32)
    ordering = jax.random.permutation(key_order, shards).astype(jnp.int32)
    following = jnp.roll(ordering, -1)
    plus_one = (shard_ids[None, :] == ordering[:, None]).astype(jnp.int32)
    minus_one = (shard_ids[None, :] == following[:, None]).astype(jnp.int32)
    counts = share_count * (1 + plus_one - minus_one)

    def spread(count_row):
        return jnp.repeat(shard_ids, count_row, total_repeat_length=TOK_DEV)
    destination = jax.vmap(spread)(counts).reshape(-1).astype(jnp.int32)
    matches = (destination[:, None] == shard_ids[None, :]).astype(jnp.int32)
    within = jnp.sum(jnp.cumsum(matches, axis=0) * matches, axis=1) - 1
    placements = jax.vmap(lambda single: jax.random.permutation(single, TOK_DEV))(jax.random.split(key_place, shards)).astype(jnp.int32)
    target = destination * TOK_DEV + placements[destination, within]
    shuffles = jax.vmap(lambda single: jax.random.permutation(single, TOK_DEV))(jax.random.split(key_slots, shards)).astype(jnp.int32)
    arranged = jnp.take_along_axis(target.reshape(shards, TOK_DEV), shuffles, axis=1)
    return arranged.reshape(-1).astype(jnp.int32)


def draw_long_group_filter(key, part):
    key_taps, key_rate, key_scale = jax.random.split(key, 3)
    lags = jnp.arange(TAPS, dtype=jnp.float32)
    rates = jnp.exp(jax.random.uniform(key_rate, (GROUPS, 1), jnp.float32, math.log(8.0), math.log(512.0)))
    values = jnp.clip(jax.random.normal(key_taps, (GROUPS, TAPS), jnp.float32), -4.0, 4.0)
    envelope = jnp.exp(-lags[None, :] / rates)
    scales = jnp.exp(jax.random.uniform(key_scale, (GROUPS, 1), jnp.float32, math.log(0.5), math.log(2.0)))
    filtered = values * envelope * scales / jnp.sqrt(jnp.sum(envelope * envelope, axis=1, keepdims=True))
    return filtered.astype(jnp.bfloat16)


def shard_levels(own_key, dims, cuts, low, top_value):
    loudness = 1.0
    for dim, shards_of in cuts:
        heights = jax.random.uniform(jax.random.fold_in(jax.random.fold_in(own_key, 6), dim), (shards_of,), jnp.float32, low / len(cuts), top_value / len(cuts))
        loudness = loudness * jnp.repeat(jnp.exp(heights), dims[dim] // shards_of).reshape((-1,) + (1,) * (len(dims) - 1 - dim))
    return loudness


def split_up(count, total, bound, slope):
    loads = [(1 << 20) // math.isqrt(grade ** slope) + 1 for grade in range(2, count + 1)]
    surplus, holding = total - bound - (count - 1), [1] * (count - 1)
    while surplus > 0:
        movable = [i for i in range(count - 1) if holding[i] < bound]
        pool, remaining = sum([loads[i] for i in movable]), surplus
        for i in movable:
            addition = min(bound - holding[i], max(1, remaining * loads[i] // pool), surplus)
            holding[i] = holding[i] + addition
            surplus = surplus - addition
    return np.array([bound] + holding)


def ragged(key, amount, total, most, lean):
    if amount == 2:
        one = jax.random.randint(key, (), max(1, total - most), min(most, total - 1) + 1)
        return jnp.stack([one, total - one])
    lengths = jnp.asarray(split_up(amount, total, most, lean), jnp.int32)
    couples = (amount - 1) // 2
    donor, receiver = lengths[1:1 + 2 * couples:2], lengths[2:2 + 2 * couples:2]
    room = jnp.minimum(donor - 1, most - receiver)
    passed = jax.random.randint(jax.random.fold_in(key, 1), (couples,), 0, 1 << 20) % (room + 1)
    lengths = lengths.at[1:1 + 2 * couples:2].set(donor - passed).at[2:2 + 2 * couples:2].set(receiver + passed)
    return lengths[jax.random.permutation(jax.random.fold_in(key, 2), amount)]


def noise(rng, dims, scale, most, cuts=(), kind=jnp.bfloat16):
    drawn = jax.random.normal(rng, dims, jnp.float32) * scale
    if len(cuts) > 0:
        drawn = shard_levels(rng, dims, cuts, -0.22, 0.18) * drawn
    return jnp.clip(drawn, min=-most, max=most).astype(kind)


def setup_inputs(seed: int = 0) -> dict:
    keys = jax.random.split(jax.random.key(seed), 11)
    tokens = noise(keys[0], (WINDOW, MIXER_WIDTH), 1.0, 6.0, ((0, 32), (1, 8)))
    frozen = noise(keys[1], (WINDOW, 3, MIXER_WIDTH), 0.5, 3.0, ((0, 32), (2, 8)))
    cotangent = noise(keys[2], (WINDOW, MIXER_WIDTH), 0.02, 0.119628906, ((0, 32), (1, 8)))
    adapter_down_weight = noise(keys[3], (ADAPTER_RANK, MIXER_WIDTH), MIXER_WIDTH ** -0.5, 0.0625, ((1, 8),))
    adapter_up_weight = noise(keys[4], (ADAPTER_RANK, 3, MIXER_WIDTH), (4 * ADAPTER_RANK) ** -0.5, 0.75, ((2, 8),))
    short_depthwise_filter = noise(keys[5], (SHORT_TAPS, 3, MIXER_WIDTH), SHORT_TAPS ** -0.5, 3.5, ((2, 8),))
    long_group_filter = draw_long_group_filter(jax.random.fold_in(keys[10], 71), 0)
    skip_direct_scale = noise(keys[7], (MIXER_WIDTH,), 0.5, 3.0, ((0, 8),), jnp.float32)
    document_lengths = ragged(keys[8], DOCS, WINDOW, LONGEST, 2).astype(jnp.int32)
    window_row_position = draw_window_row_position(jax.random.fold_in(keys[10], 71), 0)
    return dict(tokens=tokens, frozen=frozen, cotangent=cotangent, adapter_down_weight=adapter_down_weight, adapter_up_weight=adapter_up_weight, short_depthwise_filter=short_depthwise_filter, long_group_filter=long_group_filter, skip_direct_scale=skip_direct_scale, document_lengths=document_lengths, window_row_position=window_row_position)


def doc_offsets(positions, document_lengths):
    doc_ends = jnp.cumsum(document_lengths).astype(jnp.int32)
    starts = (doc_ends - document_lengths).astype(jnp.int32)
    clipped = jnp.maximum(positions, 0).astype(jnp.int32)
    begins = jnp.max(jnp.where(starts[None, :] <= clipped[:, None], starts[None, :], 0), axis=1)
    return (clipped - begins).astype(jnp.int32)


def tap_mask(offsets, shift_tap, ndim):
    return (shift_tap <= offsets).astype(jnp.float32).reshape((-1,) + (1,) * (ndim - 1))


def rounded_length(value):
    return lax.optimization_barrier(value.astype(jnp.bfloat16)).astype(jnp.float32)


def short_forward(pre_rows, filter_taps, offsets):
    length = pre_rows.shape[0]
    taps = filter_taps.shape[0]
    reach = taps - 1
    padded = jnp.concatenate([jnp.zeros((reach,) + pre_rows.shape[1:], jnp.float32), pre_rows])
    running = jnp.zeros(pre_rows.shape, jnp.float32)
    for shift_tap in range(taps):
        running = running + filter_taps[shift_tap] * padded[reach - shift_tap:reach - shift_tap + length] * tap_mask(offsets, shift_tap, pre_rows.ndim)
    return running


def short_adjoint(back_rows, filter_taps, offsets):
    length = back_rows.shape[0]
    taps = filter_taps.shape[0]
    reach = taps - 1
    running = jnp.zeros(back_rows.shape, jnp.float32)
    for shift_tap in range(taps):
        masked = back_rows * tap_mask(offsets, shift_tap, back_rows.ndim)
        padded = jnp.concatenate([masked, jnp.zeros((reach,) + back_rows.shape[1:], jnp.float32)])
        running = running + filter_taps[shift_tap] * padded[shift_tap:shift_tap + length]
    return running


def short_gradient(back_rows, pre_rows, offsets, taps):
    length = pre_rows.shape[0]
    reach = taps - 1
    padded = jnp.concatenate([jnp.zeros((reach,) + pre_rows.shape[1:], jnp.float32), pre_rows])
    collected = []
    for shift_tap in range(taps):
        shifted = padded[reach - shift_tap:reach - shift_tap + length]
        collected.append(jnp.sum(back_rows * shifted * tap_mask(offsets, shift_tap, pre_rows.ndim), axis=0))
    return jnp.stack(collected)


def long_forward(product_rows, filter_bank, offsets):
    length, channels = product_rows.shape
    padded = jnp.concatenate([jnp.zeros((128, channels), jnp.float32), product_rows])

    def one_tap(shift_tap, running):
        shift_tap = shift_tap.astype(jnp.int32)
        column = jnp.repeat(lax.dynamic_index_in_dim(filter_bank, shift_tap, 1, keepdims=False), 16)
        shifted = lax.dynamic_slice_in_dim(padded, (128 - shift_tap).astype(jnp.int32), length, 0)
        tap_gate = (shift_tap <= offsets).astype(jnp.float32)[:, None]
        return running + column[None, :] * shifted * tap_gate

    return lax.fori_loop(0, 128, one_tap, jnp.zeros((length, channels), jnp.float32))


def long_adjoint(back_rows, filter_bank, offsets):
    length, channels = back_rows.shape

    def one_tap(shift_tap, running):
        shift_tap = shift_tap.astype(jnp.int32)
        column = jnp.repeat(lax.dynamic_index_in_dim(filter_bank, shift_tap, 1, keepdims=False), 16)
        tap_gate = (shift_tap <= offsets).astype(jnp.float32)[:, None]
        padded = jnp.concatenate([back_rows * tap_gate, jnp.zeros((128, channels), jnp.float32)])
        shifted = lax.dynamic_slice_in_dim(padded, shift_tap, length, 0)
        return running + column[None, :] * shifted

    return lax.fori_loop(0, 128, one_tap, jnp.zeros((length, channels), jnp.float32))


def long_gradient(back_rows, product_rows, offsets):
    length, channels = product_rows.shape
    padded = jnp.concatenate([jnp.zeros((128, channels), jnp.float32), product_rows])

    def one_tap(shift_tap, running):
        shift_tap = shift_tap.astype(jnp.int32)
        shifted = lax.dynamic_slice_in_dim(padded, (128 - shift_tap).astype(jnp.int32), length, 0)
        tap_gate = (shift_tap <= offsets).astype(jnp.float32)[:, None]
        per_channel = jnp.sum(back_rows * shifted * tap_gate, axis=0)
        per_group = per_channel.reshape(channels // 16, 16).sum(axis=1)
        return lax.dynamic_update_slice(running, per_group[:, None], (jnp.int32(0), shift_tap))

    return lax.fori_loop(0, 128, one_tap, jnp.zeros((channels // 16, 128), jnp.float32))


def reference(tokens, frozen, cotangent, adapter_down_weight, adapter_up_weight, short_depthwise_filter, long_group_filter, skip_direct_scale, document_lengths, window_row_position):
    width_tile_block = MIXER_WIDTH // N_TP
    rank_total = adapter_down_weight.shape[0]
    taps = short_depthwise_filter.shape[0]
    packed_token_rows = jnp.zeros((WINDOW, MIXER_WIDTH), jnp.bfloat16).at[window_row_position].set(tokens)
    packed_frozen = jnp.zeros((WINDOW, 3, MIXER_WIDTH), jnp.bfloat16).at[window_row_position].set(frozen)
    offsets = doc_offsets(jnp.arange(WINDOW, dtype=jnp.int32), document_lengths)
    lowrank_product = jnp.dot(adapter_down_weight, packed_token_rows.T, preferred_element_type=jnp.float32).astype(jnp.bfloat16)
    lowrank_single_float = lowrank_product.astype(jnp.float32)

    frozen_parts = packed_frozen.reshape(WINDOW, 3, N_TP, width_tile_block).transpose(2, 0, 1, 3)
    cot_parts = cotangent.reshape(WINDOW, N_TP, width_tile_block).transpose(1, 0, 2)
    up_weight_pieces = adapter_up_weight.reshape(rank_total, 3, N_TP, width_tile_block).transpose(2, 0, 1, 3)
    short_parts = short_depthwise_filter.reshape(taps, 3, N_TP, width_tile_block).transpose(2, 0, 1, 3)
    long_parts = long_group_filter.reshape(N_TP, GROUPS // N_TP, 128)
    skip_parts = skip_direct_scale.reshape(N_TP, width_tile_block)

    def one_block(carried_state, pieces):
        frozen_piece, cot_part, up_part, short_part, long_part, skip_part = pieces
        up_weight_single_float = up_part.astype(jnp.float32)
        short_float = short_part.astype(jnp.float32)
        long_float = long_part.astype(jnp.float32)
        before_convolution = rounded_length(frozen_piece.astype(jnp.float32) + jnp.einsum('ed,ejg->djg', lowrank_single_float, up_weight_single_float))
        post_conv = rounded_length(short_forward(before_convolution, short_float, offsets))
        query_rows = post_conv[:, 0]
        key_rows = post_conv[:, 1]
        value_rows = post_conv[:, 2]
        product = rounded_length(key_rows * value_rows)
        convolved = long_forward(product, long_float, offsets)
        mixer_part = (query_rows * (convolved + skip_part[None, :] * product)).astype(jnp.bfloat16)
        grad_float = cot_part.astype(jnp.float32)
        gated_back = grad_float * query_rows
        back_conv = rounded_length(gated_back)
        product_back = long_adjoint(back_conv, long_float, offsets) + skip_part[None, :] * gated_back
        grad_long_part = long_gradient(back_conv, product, offsets)
        grad_skip_part = jnp.sum(gated_back * product, axis=0)
        query_back = grad_float * (convolved + skip_part[None, :] * product)
        back_post = rounded_length(jnp.stack([query_back, product_back * value_rows, product_back * key_rows], axis=1))
        gradient_before_filter = rounded_length(short_adjoint(back_post, short_float, offsets))
        grad_short_part = short_gradient(back_post, before_convolution, offsets, taps)
        up_gradient_piece = jnp.einsum('kp,pme->kme', lowrank_single_float, gradient_before_filter)
        carried_state = carried_state + jnp.einsum('ldx,idx->li', up_weight_single_float, gradient_before_filter)
        return carried_state, (mixer_part, up_gradient_piece, grad_short_part, grad_long_part, grad_skip_part)

    start = jnp.zeros((rank_total, WINDOW), jnp.float32)
    carried_state, stacked = lax.scan(one_block, start, (frozen_parts, cot_parts, up_weight_pieces, short_parts, long_parts, skip_parts))
    mixer_parts, grad_up_parts, grad_short_parts, grad_long_parts, grad_skip_parts = stacked
    back_low = carried_state.astype(jnp.bfloat16)
    grad_down = jnp.dot(back_low, packed_token_rows, preferred_element_type=jnp.float32)
    mixer_out = mixer_parts.transpose(1, 0, 2).reshape(WINDOW, MIXER_WIDTH)
    up_gradient = grad_up_parts.transpose(1, 2, 0, 3).reshape(rank_total, 3, MIXER_WIDTH)
    grad_short = grad_short_parts.transpose(1, 2, 0, 3).reshape(taps, 3, MIXER_WIDTH)
    grad_long = grad_long_parts.reshape(GROUPS, 128)
    grad_skip = grad_skip_parts.reshape(MIXER_WIDTH)
    return (mixer_out, grad_down, up_gradient, grad_short, grad_long, grad_skip)
```

```python
import jax
import jax.numpy as jnp
from jax import lax
from jax.experimental import pallas as pl
from jax.experimental.pallas import tpu as pltpu
from jax.sharding import PartitionSpec as P

BF = jnp.bfloat16
F32 = jnp.float32
I32 = jnp.int32


def whole(kernel, outs, scratch=(), flops=0, nbytes=0):
    def call(*args):
        return pl.pallas_call(
            kernel,
            out_shape=tuple(jax.ShapeDtypeStruct(s, d) for s, d in outs),
            in_specs=[pl.BlockSpec(memory_space=pltpu.VMEM)] * len(args),
            out_specs=tuple(pl.BlockSpec(memory_space=pltpu.VMEM) for _ in outs),
            scratch_shapes=list(scratch),
            compiler_params=pltpu.CompilerParams(vmem_limit_bytes=40 << 20),
            cost_estimate=pl.CostEstimate(flops=flops, bytes_accessed=nbytes, transcendentals=0),
        )(*args)

    return call


def dot(a, b, ca=1, cb=0):
    return lax.dot_general(a, b, (((ca,), (cb,)), ((), ())), preferred_element_type=F32)


def iota(shape, dim):
    return lax.broadcasted_iota(I32, shape, dim)


def send_kernel(pos_ref, tok_ref, frozen_ref, down_ref, out_ref, sel_ref):
    rows = pos_ref.shape[1]
    slots = sel_ref.shape[0]
    shards, cap, _ = out_ref.shape
    pos = pos_ref[...]
    dest = (pos // rows).astype(F32)
    within = (pos % rows).astype(F32)
    dest_row = jnp.broadcast_to(dest, (rows, rows))
    dest_col = dest_row.T
    earlier = (dest_row == dest_col) & (iota((rows, rows), 0) < iota((rows, rows), 1))
    rank = jnp.sum(jnp.where(earlier, 1.0, 0.0), axis=0, keepdims=True)
    slot = dest * cap + rank
    sel = jnp.where(
        iota((slots, rows), 0).astype(F32) == jnp.broadcast_to(slot, (slots, rows)), 1.0, 0.0
    ).astype(BF)
    sel_ref[...] = sel
    down = down_ref[...]
    rank_dim = down.shape[0]
    down3 = jnp.concatenate([down, down, down, jnp.zeros((128 - 3 * rank_dim, down.shape[1]), BF)])
    low = dot(tok_ref[...], down3, 1, 1)
    high = low.astype(BF).astype(F32)
    rest = low - high
    mid = rest.astype(BF).astype(F32)
    tail = rest - mid
    lane = iota((rows, 128), 1)
    within_col = jnp.broadcast_to(within, (128, rows)).T
    extra = jnp.where(
        lane < rank_dim,
        high,
        jnp.where(
            lane < 2 * rank_dim,
            mid,
            jnp.where(
                lane < 3 * rank_dim,
                tail,
                jnp.where(lane == 48, within_col, jnp.where(lane == 49, 1.0, 0.0)),
            ),
        ),
    )
    parts, _, chans = frozen_ref.shape
    out_ref[:, :, parts * chans :] = (
        dot(sel, extra.astype(BF)).astype(BF).reshape(shards, cap, 128)
    )
    for a in range(parts):
        for c in range(0, chans, 256):
            out_ref[:, :, a * chans + c : a * chans + c + 256] = (
                dot(sel, frozen_ref[a, :, c : c + 256]).astype(BF).reshape(shards, cap, 256)
            )


def send_tokens_kernel(sel_ref, tok_ref, out_ref):
    shards, cap, chans = out_ref.shape
    for c in range(0, chans, 256):
        out_ref[:, :, c : c + 256] = (
            dot(sel_ref[...], tok_ref[:, c : c + 256]).astype(BF).reshape(shards, cap, 256)
        )


def place_kernel(got_ref, place_ref, low_ref):
    shards, cap, width = got_ref.shape
    slots = shards * cap
    copies, rank_dim, rows = low_ref.shape
    extra = got_ref[:, :, width - 128 :].reshape(slots, 128)
    target = jnp.where(extra[:, 49:50].astype(F32) > 0.5, extra[:, 48:49].astype(F32), -1.0)
    place_t = jnp.where(
        jnp.broadcast_to(target, (slots, rows)) == iota((slots, rows), 1).astype(F32), 1.0, 0.0
    )
    place = place_t.T.astype(BF)
    place_ref[...] = place
    split = dot(place, extra)
    split_t = split.T
    low = split_t[:rank_dim] + split_t[rank_dim : 2 * rank_dim] + split_t[2 * rank_dim : 3 * rank_dim]
    for t in range(copies):
        low_ref[t] = low


def pack_kernel(got_ref, place_ref, out_ref):
    shards, cap, width = got_ref.shape
    parts, rows, chans = out_ref.shape
    place = place_ref[...]
    for a in range(parts):
        for c in range(0, chans, 256):
            block = got_ref[:, :, a * chans + c : a * chans + c + 256].reshape(shards * cap, 256)
            out_ref[a, :, c : c + 256] = dot(place, block).astype(BF)


def pre_kernel(packed_ref, lows_ref, up_ref, pre_ref, edge_ref, low_ref):
    parts, rows, chans = packed_ref.shape
    total = lows_ref[0]
    for t in range(1, lows_ref.shape[0]):
        total = total + lows_ref[t]
    low = total.astype(BF)
    low_ref[...] = low
    low_t = total.T.astype(BF)
    edge_ref[...] = jnp.zeros_like(edge_ref)
    for a in range(parts):
        for c in range(0, chans, 256):
            cols = slice(c, c + 256)
            value = packed_ref[a, :, cols].astype(F32) + dot(low_t, up_ref[a, :, cols])
            pre_ref[a, :, cols] = value.astype(BF)
            edge_ref[2 * a : 2 * a + 2, cols] = value[rows - 2 :]


def shifted_down(value, edge0, edge1):
    row = iota(value.shape, 0)
    one = jnp.where(row == 0, edge1, pltpu.roll(value, 1, 0))
    two = jnp.where(row == 0, edge0, jnp.where(row == 1, edge1, pltpu.roll(value, 2, 0)))
    return one, two


def post_kernel(pre_ref, edge_ref, taps_ref, off_ref, cot_ref, post_ref, x_ref, b_ref, xe_ref, be_ref):
    parts, rows, chans = pre_ref.shape
    mask1 = jnp.where(off_ref[:rows] >= 1.0, 1.0, 0.0)
    mask2 = jnp.where(off_ref[:rows] >= 2.0, 1.0, 0.0)

    def chunk(i, carry):
        cols = pl.ds(pl.multiple_of(i * 128, 128), 128)
        made = []
        for a in range(parts):
            value = pre_ref[a, :, cols].astype(F32)
            one, two = shifted_down(
                value, edge_ref[2 * a : 2 * a + 1, cols], edge_ref[2 * a + 1 : 2 * a + 2, cols]
            )
            total = (
                taps_ref[a : a + 1, cols] * value
                + taps_ref[parts + a : parts + a + 1, cols] * one * mask1
                + taps_ref[2 * parts + a : 2 * parts + a + 1, cols] * two * mask2
            ).astype(BF)
            post_ref[a, :, cols] = total
            made.append(total.astype(F32))
        product = (made[1] * made[2]).astype(BF)
        back = (cot_ref[:, cols].astype(F32) * made[0]).astype(BF)
        x_ref[:, cols] = product
        b_ref[:, cols] = back
        xe_ref[:, cols] = product[rows - 128 :]
        be_ref[:, cols] = back[:128]
        return carry

    lax.fori_loop(0, chans // 128, chunk, 0)


def conv_kernel(
    x_ref, xh_ref, b_ref, bh_ref, post_ref, cot_ref, skip_ref, filt_ref, offc_ref, offr_ref,
    mixer_ref, backpost_ref, edge_ref, long_ref, gskip_ref,
    mfwd_ref, madj_ref, mpair_ref, frow_ref, grow_ref, fwd_ref, adj_ref, lhs_ref, bm_ref, rf_ref, ra_ref, rp_ref,
):
    rows, chans = x_ref.shape
    blocks = rows // 128
    sub, lane = iota((128, 128), 0), iota((128, 128), 1)
    turn = jnp.where(sub + lane == 127, 1.0, 0.0).astype(BF)
    for b in range(blocks):
        first = 128 * b
        begin_col = (first + sub).astype(F32) - offc_ref[first : first + 128]
        own = (lane <= sub) & ((first + lane).astype(F32) >= begin_col)
        prev = (lane > sub) & ((first - 128 + lane).astype(F32) >= begin_col)
        prev, own = jnp.where(prev, 1.0, 0.0), jnp.where(own, 1.0, 0.0)
        mfwd_ref[b, :, :128] = prev.astype(BF)
        mfwd_ref[b, :, 128:] = own.astype(BF)
        mpair_ref[b, :, :128] = dot(turn, prev.astype(BF))
        mpair_ref[b, :, 128:] = dot(turn, own.astype(BF))
        row0 = jnp.broadcast_to(offr_ref[:, first : first + 128], (128, 128))
        row1 = jnp.broadcast_to(offr_ref[:, first + 128 : first + 256], (128, 128))
        begin0 = (first + lane).astype(F32) - row0
        begin1 = (first + 128 + lane).astype(F32) - row1
        at = (first + sub).astype(F32)
        same = (sub <= lane) & (at >= begin0)
        after = (lane < sub) & (at >= begin1)
        madj_ref[b, :, :128] = jnp.where(same, 1.0, 0.0).astype(BF)
        madj_ref[b, :, 128:] = jnp.where(after, 1.0, 0.0).astype(BF)
    filt = filt_ref[...]
    flip = jnp.where((sub + lane) % 128 == 0, 1.0, 0.0).astype(BF)
    frow_ref[...] = filt.astype(F32)
    grow_ref[...] = dot(filt, flip)

    def chunk(i, carry):
        cols = pl.ds(pl.multiple_of(i * 128, 128), 128)
        for g in range(8):
            f_row = jnp.broadcast_to(frow_ref[pl.ds(i * 8 + g, 1), :], (128, 128))
            g_row = jnp.broadcast_to(grow_ref[pl.ds(i * 8 + g, 1), :], (128, 128))
            circ = pltpu.roll(f_row, 0, 1, stride=1, stride_axis=0).astype(BF)
            circ_t = pltpu.roll(g_row, 0, 1, stride=1, stride_axis=0).astype(BF)
            two, two_t = jnp.concatenate([circ, circ], 1), jnp.concatenate([circ_t, circ_t], 1)
            for b in range(blocks):
                fwd_ref[b, 128 * g : 128 * g + 128] = two_t * mfwd_ref[b]
                adj_ref[b, 128 * g : 128 * g + 128] = two * madj_ref[b]
        x_win = jnp.concatenate([xh_ref[:, cols], x_ref[:, cols]])
        b_win = jnp.concatenate([b_ref[:, cols], bh_ref[:, cols]])
        lane_group = lane // 16
        for b in range(blocks):
            xw = x_win[128 * b : 128 * b + 256]
            rf_ref[b] = dot(fwd_ref[b], xw)
            ra_ref[b] = dot(adj_ref[b], b_win[128 * b : 128 * b + 256])
            back = dot(turn, b_win[128 * b : 128 * b + 128])
            for g in range(8):
                lhs_ref[128 * g : 128 * g + 128] = jnp.where(lane_group == g, back, 0.0).astype(BF)
            rp_ref[b] = dot(lhs_ref[...], xw, 1, 1)
        for g in range(8):
            part = jnp.zeros((128, 128), F32)
            for b in range(blocks):
                pair = rp_ref[b, 128 * g : 128 * g + 128] * mpair_ref[b]
                part = part + pair[:, :128] + pair[:, 128:]
            part = pltpu.roll(part, 0, 1, stride=1, stride_axis=0)
            long_ref[pl.ds(i * 8 + g, 1), :] = jnp.sum(part, axis=0, keepdims=True)
        skip = skip_ref[:, cols]
        gsum = jnp.zeros((1, 128), F32)
        for b in range(blocks):
            conv = jnp.zeros((128, 128), F32)
            adj = jnp.zeros((128, 128), F32)
            for g in range(8):
                conv = jnp.where(lane_group == g, rf_ref[b, 128 * g : 128 * g + 128], conv)
                adj = jnp.where(lane_group == g, ra_ref[b, 128 * g : 128 * g + 128], adj)
            at = slice(128 * b, 128 * b + 128)
            query, key, value = (post_ref[a, at, cols].astype(F32) for a in range(3))
            product = x_ref[at, cols].astype(F32)
            grad = cot_ref[at, cols].astype(F32)
            direct = conv + skip * product
            mixer_ref[at, cols] = (query * direct).astype(BF)
            gated = grad * query
            back = adj + skip * gated
            gsum = gsum + jnp.sum(gated * product, axis=0, keepdims=True)
            for a, post in enumerate((grad * direct, back * value, back * key)):
                post = post.astype(BF)
                backpost_ref[a, at, cols] = post
                if b == 0:
                    edge_ref[2 * a : 2 * a + 2, cols] = post[:2].astype(F32)
        gskip_ref[:, cols] = gsum
        return carry

    edge_ref[...] = jnp.zeros_like(edge_ref)
    lax.fori_loop(0, chans // 128, chunk, 0)


def back_kernel(
    backpost_ref, nedge_ref, pre_ref, pedge_ref, taps_ref, off_ref, low_ref, up_ref,
    upgrad_ref, short_ref, backlow_ref,
):
    parts, rows, chans = pre_ref.shape
    rank_dim = low_ref.shape[0]
    mask1 = jnp.where(off_ref[:rows] >= 1.0, 1.0, 0.0)
    mask2 = jnp.where(off_ref[:rows] >= 2.0, 1.0, 0.0)
    next1 = jnp.where(off_ref[rows : rows + 8] >= 1.0, 1.0, 0.0)
    next2 = jnp.where(off_ref[rows : rows + 8] >= 2.0, 1.0, 0.0)
    low = low_ref[...]
    row = iota((rows, 128), 0)

    def chunk(i, total):
        cols = pl.ds(pl.multiple_of(i * 128, 128), 128)
        for a in range(parts):
            post = backpost_ref[a, :, cols].astype(F32)
            edge0 = nedge_ref[2 * a : 2 * a + 1, cols]
            edge1 = nedge_ref[2 * a + 1 : 2 * a + 2, cols]
            post1, post2 = post * mask1, post * mask2
            up1 = jnp.where(row == rows - 1, edge0 * next1[0:1], pltpu.roll(post1, rows - 1, 0))
            up2 = jnp.where(
                row == rows - 2,
                edge0 * next2[0:1],
                jnp.where(row == rows - 1, edge1 * next2[1:2], pltpu.roll(post2, rows - 2, 0)),
            )
            back_pre = (
                taps_ref[a : a + 1, cols] * post
                + taps_ref[parts + a : parts + a + 1, cols] * up1
                + taps_ref[2 * parts + a : 2 * parts + a + 1, cols] * up2
            ).astype(BF)
            pre = pre_ref[a, :, cols].astype(F32)
            one, two = shifted_down(
                pre, pedge_ref[2 * a : 2 * a + 1, cols], pedge_ref[2 * a + 1 : 2 * a + 2, cols]
            )
            short_ref[a : a + 1, cols] = jnp.sum(post * pre, axis=0, keepdims=True)
            short_ref[parts + a : parts + a + 1, cols] = jnp.sum(post1 * one, axis=0, keepdims=True)
            short_ref[2 * parts + a : 2 * parts + a + 1, cols] = jnp.sum(
                post2 * two, axis=0, keepdims=True
            )
            upgrad_ref[a, :, cols] = dot(low, back_pre)
            total = total + dot(up_ref[a, :, cols], back_pre, 1, 1)
        return total

    short_ref[...] = jnp.zeros_like(short_ref)
    total = lax.fori_loop(0, chans // 128, chunk, jnp.zeros((rank_dim, rows), F32))
    for t in range(backlow_ref.shape[0]):
        backlow_ref[t] = total


def gather_kernel(lows_ref, got_ref, place_ref, upgrad_ref, short_ref, gskip_ref, long_ref, out_ref):
    shards, cap, chans = got_ref.shape
    total = lows_ref[0]
    for t in range(1, lows_ref.shape[0]):
        total = total + lows_ref[t]
    low = total.astype(BF)
    placed = dot(low, place_ref[...]).astype(BF)
    tiles = chans // 128
    for i in range(tiles):
        cols = slice(128 * i, 128 * i + 128)
        down = dot(placed, got_ref[:, :, cols].reshape(shards * cap, 128))
        up = [upgrad_ref[a, :, cols] for a in range(3)]
        out_ref[i, :16] = down
        out_ref[i, 16:24] = up[0][:8]
        out_ref[tiles + i, :8] = up[0][8:]
        out_ref[tiles + i, 8:24] = up[1]
        out_ref[2 * tiles + i, :16] = up[2]
        out_ref[2 * tiles + i, 16:24] = short_ref[:8, cols]
        out_ref[3 * tiles + i, :8] = jnp.where(
            iota((8, 128), 0) == 0,
            jnp.broadcast_to(short_ref[8:9, cols], (8, 128)),
            jnp.broadcast_to(gskip_ref[:, cols], (8, 128)),
        )
        out_ref[3 * tiles + i, 8:16] = long_ref[8 * i : 8 * i + 8]
        out_ref[3 * tiles + i, 16:24] = jnp.zeros((8, 128), F32)


def sum_kernel(in_ref, out_ref):
    total = in_ref[0]
    for t in range(1, in_ref.shape[0]):
        total = total + in_ref[t]
    for t in range(out_ref.shape[0]):
        out_ref[t] = total


def spread_kernel(in_ref, down_ref, up_ref, short_ref, long_ref, gskip_ref):
    tiles = down_ref.shape[1] // 128
    flip = jnp.where(iota((128, 128), 0) + iota((128, 128), 1) == 127, 1.0, 0.0)
    for i in range(tiles):
        cols = slice(128 * i, 128 * i + 128)
        down_ref[:, cols] = in_ref[i, :16]
        up_ref[0, :8, cols] = in_ref[i, 16:24]
        up_ref[0, 8:, cols] = in_ref[tiles + i, :8]
        up_ref[1, :, cols] = in_ref[tiles + i, 8:24]
        up_ref[2, :, cols] = in_ref[2 * tiles + i, :16]
        short_ref[:8, cols] = in_ref[2 * tiles + i, 16:24]
        short_ref[8:9, cols] = in_ref[3 * tiles + i, 0:1]
        gskip_ref[:, cols] = in_ref[3 * tiles + i, 1:2]
        long_ref[8 * i : 8 * i + 8] = lax.dot_general(
            in_ref[3 * tiles + i, 8:16],
            flip,
            (((1,), (0,)), ((), ())),
            precision=lax.Precision.HIGHEST,
            preferred_element_type=F32,
        )


def swap(value, axis):
    return lax.all_to_all(value, axis, split_axis=0, concat_axis=0, tiled=True)


def neighbour(value, steps):
    count = lax.axis_size("ctx")
    pairs = [(i, i + steps) for i in range(count) if 0 <= i + steps < count]
    return lax.ppermute(value, "ctx", pairs)


def doc_offsets(positions, lengths):
    index = jnp.arange(lengths.shape[0], dtype=I32)
    starts = jnp.sum(jnp.where(index[None, :] < index[:, None], lengths[None, :], 0), axis=1)
    begins = jnp.max(jnp.where(starts[None, :] <= positions[:, None], starts[None, :], 0), axis=1)
    return positions - begins


def on_device(
    tokens,
    frozen,
    cotangent,
    adapter_down_weight,
    adapter_up_weight,
    short_depthwise_filter,
    long_group_filter,
    skip_direct_scale,
    document_lengths,
    window_row_position,
):
    rows, chans = tokens.shape
    parts = frozen.shape[1]
    rank_dim = adapter_down_weight.shape[0]
    taps = short_depthwise_filter.shape[0]
    groups = long_group_filter.shape[0]
    shards = lax.axis_size("ctx")
    columns = lax.axis_size("tp")
    cap = 2 * rows // shards
    slots = shards * cap
    frozen = frozen.transpose(1, 0, 2)
    up = adapter_up_weight.transpose(1, 0, 2)
    send, sel = whole(
        send_kernel,
        [((shards, cap, parts * chans + 128), BF), ((slots, rows), BF)],
        flops=2 * slots * rows * parts * chans,
        nbytes=5 << 20,
    )(window_row_position.reshape(1, rows), tokens, frozen, adapter_down_weight)
    got = swap(send, "ctx")

    send, sel, document_lengths, short_depthwise_filter = lax.optimization_barrier(
        (send, sel, document_lengths, short_depthwise_filter)
    )
    (send_tok,) = whole(
        send_tokens_kernel, [((shards, cap, chans), BF)], flops=2 * slots * rows * chans, nbytes=2 << 20
    )(sel, tokens)
    first = lax.axis_index("ctx") * rows
    offsets = doc_offsets(first + jnp.arange(rows + 128, dtype=I32), document_lengths).astype(F32)
    off_row = offsets.reshape(1, rows + 128)
    off_col = jnp.broadcast_to(offsets[:, None], (rows + 128, 128))
    tap_rows = short_depthwise_filter.reshape(taps * parts, chans).astype(F32)
    tap_rows = jnp.pad(tap_rows, ((0, 16 - taps * parts), (0, 0)))
    skip_row = skip_direct_scale.reshape(1, chans)

    place, low_part = whole(
        place_kernel, [((rows, slots), BF), ((columns, rank_dim, rows), F32)], flops=1 << 26, nbytes=1 << 20
    )(got)
    lows = swap(low_part, "tp")
    (packed,) = whole(
        pack_kernel, [((parts, rows, chans), BF)], flops=2 * slots * rows * parts * chans, nbytes=5 << 20
    )(got, place)
    pre, pre_edge, low = whole(
        pre_kernel,
        [((parts, rows, chans), BF), ((8, chans), F32), ((rank_dim, rows), BF)],
        flops=1 << 27,
        nbytes=4 << 20,
    )(packed, lows, up)
    send_tok, low = lax.optimization_barrier((send_tok, low))
    edge_in = neighbour(pre_edge, 1)
    post, x, back, x_tail, b_head = whole(
        post_kernel,
        [
            ((parts, rows, chans), BF),
            ((rows, chans), BF),
            ((rows, chans), BF),
            ((128, chans), BF),
            ((128, chans), BF),
        ],
        flops=1 << 25,
        nbytes=6 << 20,
    )(pre, edge_in, tap_rows, off_col, cotangent)
    got_tok = swap(send_tok, "ctx")
    x_halo = neighbour(x_tail, 1)
    b_halo = neighbour(b_head, -1)
    blocks = rows // 128
    mixer, back_post, post_edge, long_part, skip_part = whole(
        conv_kernel,
        [
            ((rows, chans), BF),
            ((parts, rows, chans), BF),
            ((8, chans), F32),
            ((groups, 128), F32),
            ((1, chans), F32),
        ],
        scratch=[
            pltpu.VMEM((blocks, 128, 256), BF),
            pltpu.VMEM((blocks, 128, 256), BF),
            pltpu.VMEM((blocks, 128, 256), F32),
            pltpu.VMEM((groups, 128), F32),
            pltpu.VMEM((groups, 128), F32),
            pltpu.VMEM((blocks, 1024, 256), BF),
            pltpu.VMEM((blocks, 1024, 256), BF),
            pltpu.VMEM((1024, 128), BF),
            pltpu.VMEM((8, 128), F32),
            pltpu.VMEM((blocks, 1024, 128), F32),
            pltpu.VMEM((blocks, 1024, 128), F32),
            pltpu.VMEM((blocks, 1024, 256), F32),
        ],
        flops=10 << 30,
        nbytes=8 << 20,
    )(x, x_halo, back, b_halo, post, cotangent, skip_row, long_group_filter, off_col, off_row)
    got_tok, post_edge = lax.optimization_barrier((got_tok, post_edge))
    edge_next = neighbour(post_edge, -1)
    up_part, short_part, back_low_part = whole(
        back_kernel,
        [
            ((parts, rank_dim, chans), F32),
            ((16, chans), F32),
            ((columns, rank_dim, rows), F32),
        ],
        flops=1 << 27,
        nbytes=6 << 20,
    )(back_post, edge_next, pre, edge_in, tap_rows, off_col, low, up)
    back_lows = swap(back_low_part, "tp")
    (pieces,) = whole(
        gather_kernel, [((shards, 24, 128), F32)], flops=1 << 26, nbytes=2 << 20
    )(back_lows, got_tok, place, up_part, short_part, skip_part, long_part)
    pieces = swap(pieces, "ctx")
    (pieces,) = whole(sum_kernel, [((shards, 24, 128), F32)], flops=1 << 20, nbytes=1 << 20)(pieces)
    pieces = swap(pieces, "ctx")
    grad_down, up_gradient, grad_short, grad_long, grad_skip = whole(
        spread_kernel,
        [
            ((rank_dim, chans), F32),
            ((parts, rank_dim, chans), F32),
            ((taps * parts, chans), F32),
            ((groups, 128), F32),
            ((1, chans), F32),
        ],
        flops=1 << 20,
        nbytes=1 << 20,
    )(pieces)
    return (
        mixer,
        grad_down,
        up_gradient.transpose(1, 0, 2),
        grad_short.reshape(taps, parts, chans),
        grad_long,
        grad_skip.reshape(chans),
    )


def solution(mesh):
    placed = (
        P("ctx", "tp"),
        P("ctx", None, "tp"),
        P("ctx", "tp"),
        P(None, "tp"),
        P(None, None, "tp"),
        P(None, None, "tp"),
        P("tp", None),
        P("tp"),
        P(),
        P("ctx"),
    )
    return jax.shard_map(
        on_device,
        mesh=mesh,
        in_specs=placed,
        out_specs=(
            P("ctx", "tp"),
            P(None, "tp"),
            P(None, None, "tp"),
            P(None, None, "tp"),
            P("tp", None),
            P("tp"),
        ),
        check_vma=False,
    )
```

```python
import jax
import jax.numpy as jnp
from jax import lax
from jax.experimental import pallas as pl
from jax.experimental.pallas import tpu as pltpu
from jax.sharding import PartitionSpec as P

BF = jnp.bfloat16
F32 = jnp.float32
I32 = jnp.int32


def whole(kernel, outs, scratch=(), flops=0, nbytes=0):
    def call(*args):
        return pl.pallas_call(
            kernel,
            out_shape=tuple(jax.ShapeDtypeStruct(s, d) for s, d in outs),
            in_specs=[pl.BlockSpec(memory_space=pltpu.VMEM)] * len(args),
            out_specs=tuple(pl.BlockSpec(memory_space=pltpu.VMEM) for _ in outs),
            scratch_shapes=list(scratch),
            compiler_params=pltpu.CompilerParams(vmem_limit_bytes=20 << 20),
            cost_estimate=pl.CostEstimate(flops=flops, bytes_accessed=nbytes, transcendentals=0),
        )(*args)

    return call


def tiled(kernel, grid, in_specs, outs, scratch, flops, nbytes, limit):
    def call(*args):
        return pl.pallas_call(
            kernel,
            grid=(grid,),
            out_shape=tuple(jax.ShapeDtypeStruct(s, d) for s, d, _, _ in outs),
            in_specs=[pl.BlockSpec(b, m) for b, m in in_specs],
            out_specs=tuple(pl.BlockSpec(b, m) for _, _, b, m in outs),
            scratch_shapes=list(scratch),
            compiler_params=pltpu.CompilerParams(
                vmem_limit_bytes=limit, dimension_semantics=("arbitrary",)
            ),
            cost_estimate=pl.CostEstimate(flops=flops, bytes_accessed=nbytes, transcendentals=0),
        )(*args)

    return call


def at2(i):
    return (0, i)


def at3(i):
    return (0, 0, i)


def fixed2(i):
    return (0, 0)


def dot(a, b, ca=1, cb=0):
    return lax.dot_general(a, b, (((ca,), (cb,)), ((), ())), preferred_element_type=F32)


def iota(shape, dim):
    return lax.broadcasted_iota(I32, shape, dim)


def send_kernel(
    pos_ref, frozen_ref, tok_ref, down_ref, out_ref, sel_ref,
    in_buf, tok_buf, out_buf, extra_buf, in_sem, out_sem,
):
    rows = pos_ref.shape[1]
    slots = sel_ref.shape[0]
    parts, shards, cap, chans = out_buf.shape
    rank_dim = down_ref.shape[0]
    loads = [pltpu.make_async_copy(tok_ref, tok_buf, in_sem.at[parts])]
    for a in range(parts):
        loads.append(pltpu.make_async_copy(frozen_ref.at[a], in_buf.at[a], in_sem.at[a]))
    for load in loads:
        load.start()
    pos = pos_ref[...]
    dest = (pos // rows).astype(F32)
    within = (pos % rows).astype(F32)
    dest_row = jnp.broadcast_to(dest, (rows, rows))
    dest_col = dest_row.T
    earlier = (dest_row == dest_col) & (iota((rows, rows), 0) < iota((rows, rows), 1))
    rank = jnp.sum(jnp.where(earlier, 1.0, 0.0), axis=0, keepdims=True)
    slot = dest * float(cap) + rank
    sel = jnp.where(
        iota((slots, rows), 0).astype(F32) == jnp.broadcast_to(slot, (slots, rows)), 1.0, 0.0
    ).astype(BF)
    sel_ref[...] = sel
    mark = jnp.where(iota((8, rows), 0) == 0, jnp.broadcast_to(within, (8, rows)), 1.0)
    loads[0].wait()
    low = dot(down_ref[...], tok_buf[...], 1, 1)
    high = low.astype(BF).astype(F32)
    rest = low - high
    mid = rest.astype(BF).astype(F32)
    extra = jnp.concatenate(
        [high, mid, rest - mid, mark, jnp.zeros((128 - 8 - 3 * rank_dim, rows), F32)]
    )
    extra_buf[...] = dot(sel, extra.T.astype(BF)).astype(BF).reshape(shards, cap, 128)
    stores = [
        pltpu.make_async_copy(
            extra_buf, out_ref.at[:, :, pl.ds(parts * chans, 128)], out_sem.at[parts]
        )
    ]
    stores[0].start()
    for a in range(parts):
        loads[1 + a].wait()
        for c in range(0, chans, 256):
            out_buf[a, :, :, c : c + 256] = (
                dot(sel, in_buf[a, :, c : c + 256]).astype(BF).reshape(shards, cap, 256)
            )
        store = pltpu.make_async_copy(
            out_buf.at[a], out_ref.at[:, :, pl.ds(a * chans, chans)], out_sem.at[a]
        )
        store.start()
        stores.append(store)
    for store in stores:
        store.wait()


def send_tokens_kernel(sel_ref, tok_ref, out_ref):
    shards, cap, chans = out_ref.shape
    for c in range(0, chans, 256):
        out_ref[:, :, c : c + 256] = (
            dot(sel_ref[...], tok_ref[:, c : c + 256]).astype(BF).reshape(shards, cap, 256)
        )


def place_kernel(extra_ref, place_ref, low_ref):
    copies, rank_dim, rows = low_ref.shape
    shards, cap, _ = extra_ref.shape
    slots = shards * cap
    extra = extra_ref[...].reshape(slots, 128)
    mark = extra[:, 3 * rank_dim : 3 * rank_dim + 2].astype(F32)
    target = jnp.where(mark[:, 1:2] > 0.5, mark[:, 0:1], -1.0)
    place_t = jnp.where(
        jnp.broadcast_to(target, (slots, rows)) == iota((slots, rows), 1).astype(F32), 1.0, 0.0
    )
    place = place_t.T.astype(BF)
    place_ref[...] = place
    split = dot(place, extra).T
    low = split[:rank_dim] + split[rank_dim : 2 * rank_dim] + split[2 * rank_dim : 3 * rank_dim]
    for t in range(copies):
        low_ref[t] = low


def shifted_down(value, edge0, edge1):
    row = iota(value.shape, 0)
    one = jnp.where(row == 0, edge1, pltpu.roll(value, 1, 0))
    two = jnp.where(row == 0, edge0, jnp.where(row == 1, edge1, pltpu.roll(value, 2, 0)))
    return one, two


def post_kernel(
    got0_ref, got1_ref, got2_ref, place_ref, lows_ref, up_ref, taps_ref, off_ref, cot_ref,
    pre_ref, post_ref, x_ref, b_ref, ahead_ref, behind_ref, low_ref,
    ahead_edge, behind_edge, low_t_ref,
):
    parts, rows, width = pre_ref.shape
    slots = place_ref.shape[1]

    @pl.when(pl.program_id(0) == 0)
    def _():
        total = lows_ref[0]
        for t in range(1, lows_ref.shape[0]):
            total = total + lows_ref[t]
        low_ref[...] = total.astype(BF)
        low_t_ref[...] = total.T.astype(BF)

    off = jnp.concatenate([off_ref[:rows]] * (width // 128), 1)
    mask1 = jnp.where(off >= 1.0, 1.0, 0.0)
    mask2 = jnp.where(off >= 2.0, 1.0, 0.0)
    ahead_edge[...] = jnp.zeros_like(ahead_edge)
    behind_edge[...] = jnp.zeros_like(behind_edge)
    nothing = jnp.zeros((1, width), F32)
    made = []
    for a, got_ref in enumerate((got0_ref, got1_ref, got2_ref)):
        value = dot(place_ref[...], got_ref[...].reshape(slots, width)) + dot(low_t_ref[...], up_ref[a])
        value = value.astype(BF)
        pre_ref[a] = value
        value = value.astype(F32)
        ahead_edge[2 * a : 2 * a + 2] = value[rows - 2 :]
        behind_edge[2 * a : 2 * a + 2] = value[:2]
        one, two = shifted_down(value, nothing, nothing)
        total = (
            taps_ref[a : a + 1] * value
            + taps_ref[parts + a : parts + a + 1] * one * mask1
            + taps_ref[2 * parts + a : 2 * parts + a + 1] * two * mask2
        ).astype(BF)
        post_ref[a] = total
        made.append(total.astype(F32))
    product = (made[1] * made[2]).astype(BF)
    grad = cot_ref[...].astype(F32)
    back = (grad * made[0]).astype(BF)
    x_ref[...] = product
    b_ref[...] = back
    ahead_ref[:128] = product[rows - 128 :]
    behind_ref[:128] = back[:128]
    behind_edge[6:8] = grad[:2]
    behind_edge[8:9] = back[128:144].astype(F32)[:1]
    ahead_ref[128:] = ahead_edge[...].astype(BF)
    behind_ref[128:] = behind_edge[...].astype(BF)


def main_kernel(
    pre_ref, post_ref, x_ref, b_ref, prev_ref, next_ref, cot_ref, taps_ref, skip_ref, filt_ref,
    offc_ref, offr_ref, low_ref, up_ref,
    mixer_ref, piece_ref, backlow_ref,
    mfwd_ref, madj_ref, mpair_ref, frow_ref, grow_ref, fwd_ref, adj_ref, lhs_ref, rf_ref, ra_ref, rp_ref, bp_ref, total_ref,
):
    parts, rows, _ = pre_ref.shape
    step = pl.program_id(0)
    rank_dim = low_ref.shape[0]
    blocks = rows // 128
    sub, lane = iota((128, 128), 0), iota((128, 128), 1)
    turn = jnp.where(sub + lane == 127, 1.0, 0.0).astype(BF)
    @pl.when(step == 0)
    def _():
        total_ref[...] = jnp.zeros_like(total_ref)
        for b in range(blocks + 1):
            first = 128 * b
            tall = 128 if b < blocks else 16
            begin_col = (first + sub).astype(F32) - offc_ref[first : first + 128]
            own = (lane <= sub) & ((first + lane).astype(F32) >= begin_col)
            prev = (lane > sub) & ((first - 128 + lane).astype(F32) >= begin_col)
            prev, own = jnp.where(prev, 1.0, 0.0).astype(BF), jnp.where(own, 1.0, 0.0).astype(BF)
            mfwd_ref[first : first + tall, :128] = prev[:tall]
            mfwd_ref[first : first + tall, 128:] = own[:tall]
            if b < blocks:
                mpair_ref[b, :, :128] = dot(turn, prev)
                mpair_ref[b, :, 128:] = dot(turn, own)
            row0 = jnp.broadcast_to(offr_ref[:, first : first + 128], (128, 128))
            row1 = jnp.broadcast_to(offr_ref[:, first + 128 : first + 256], (128, 128))
            begin0 = (first + lane).astype(F32) - row0
            begin1 = (first + 128 + lane).astype(F32) - row1
            at = (first + sub).astype(F32)
            same = jnp.where((sub <= lane) & (at >= begin0), 1.0, 0.0).astype(BF)
            after = jnp.where((lane < sub) & (at >= begin1), 1.0, 0.0).astype(BF)
            madj_ref[first : first + tall, :128] = same[:tall]
            madj_ref[first : first + tall, 128:] = after[:tall]

    filt = filt_ref[...]
    flip = jnp.where((sub + lane) % 128 == 0, 1.0, 0.0).astype(BF)
    frow_ref[...] = filt.astype(F32)
    grow_ref[...] = dot(filt, flip)
    mask1 = jnp.where(offc_ref[:rows] >= 1.0, 1.0, 0.0)
    mask2 = jnp.where(offc_ref[:rows] >= 2.0, 1.0, 0.0)
    next1 = jnp.where(offc_ref[rows : rows + 16] >= 1.0, 1.0, 0.0)
    next2 = jnp.where(offc_ref[rows : rows + 16] >= 2.0, 1.0, 0.0)
    low = low_ref[...]
    row = iota((rows, 128), 0)
    top = iota((16, 128), 0) < 2
    lane_group = lane // 16
    piece_ref[...] = jnp.zeros_like(piece_ref)

    def tap(s, a):
        return taps_ref[s * parts + a : s * parts + a + 1]

    for g in range(8):
        f_row = jnp.broadcast_to(frow_ref[g : g + 1, :], (128, 128))
        g_row = jnp.broadcast_to(grow_ref[g : g + 1, :], (128, 128))
        circ = pltpu.roll(f_row, 0, 1, stride=1, stride_axis=0).astype(BF)
        circ_t = pltpu.roll(g_row, 0, 1, stride=1, stride_axis=0).astype(BF)
        two, two_t = jnp.concatenate([circ, circ], 1), jnp.concatenate([circ_t, circ_t], 1)
        for b in range(blocks + 1):
            tall = 128 if b < blocks else 16
            at = 1024 * b + tall * g
            fwd_ref[at : at + tall] = two_t[:tall] * mfwd_ref[128 * b : 128 * b + tall]
            adj_ref[at : at + tall] = two[:tall] * madj_ref[128 * b : 128 * b + tall]
    pedge = prev_ref[128:].astype(F32)
    nedge = next_ref[128:].astype(F32)
    heads, after = [], []
    for a in range(parts):
        head = pre_ref[a, :16].astype(F32)
        one, two = shifted_down(head, pedge[2 * a : 2 * a + 1], pedge[2 * a + 1 : 2 * a + 2])
        heads.append(
            (tap(0, a) * head + tap(1, a) * one * mask1[:16] + tap(2, a) * two * mask2[:16]).astype(BF)
        )
        tail = pre_ref[a, rows - 16 :].astype(F32)
        head = nedge if a == 0 else pltpu.roll(nedge, 16 - 2 * a, 0)
        one, two = shifted_down(head, tail[14:15], tail[15:16])
        after.append(
            (tap(0, a) * head + tap(1, a) * one * next1 + tap(2, a) * two * next2)
            .astype(BF)
            .astype(F32)
        )
    posts = [jnp.concatenate([heads[a], post_ref[a, 16:]]) for a in range(parts)]
    x_head = (heads[1].astype(F32) * heads[2].astype(F32)).astype(BF)
    b_head = (cot_ref[:16].astype(F32) * heads[0].astype(F32)).astype(BF)
    x_next = jnp.where(top, after[1] * after[2], 0.0).astype(BF)
    cot_next = pltpu.roll(nedge, 10, 0)
    b_next = jnp.where(top, cot_next * after[0], next_ref[:16].astype(F32)).astype(BF)
    b_last = jnp.where(iota((16, 128), 0) == 0, pltpu.roll(nedge, 8, 0), 0.0).astype(BF)
    blank = jnp.zeros((112, 128), BF)
    x_own = jnp.concatenate([x_head, x_ref[16:]])
    x_win = jnp.concatenate([prev_ref[:128], x_own, x_next, blank])
    b_win = jnp.concatenate(
        [b_head, b_ref[16:], b_next, next_ref[16:128], b_last, blank]
    )
    for b in range(blocks + 1):
        at = slice(1024 * b, 1024 * b + (1024 if b < blocks else 128))
        xw = x_win[128 * b : 128 * b + 256]
        rf_ref[at] = dot(fwd_ref[at], xw)
        ra_ref[at] = dot(adj_ref[at], b_win[128 * b : 128 * b + 256])
        if b < blocks:
            back = dot(turn, b_win[128 * b : 128 * b + 128])
            for g in range(8):
                lhs_ref[128 * g : 128 * g + 128] = jnp.where(lane_group == g, back, 0.0).astype(BF)
            rp_ref[b] = dot(lhs_ref[...], xw, 1, 1)
    for g in range(8):
        part = jnp.zeros((128, 128), F32)
        for b in range(blocks):
            pair = rp_ref[b, 128 * g : 128 * g + 128] * mpair_ref[b]
            part = part + pair[:, :128] + pair[:, 128:]
        part = pltpu.roll(part, 0, 1, stride=1, stride_axis=0)
        piece_ref[3, 0, 8 + g : 9 + g] = jnp.sum(part, axis=0, keepdims=True)
    skip = skip_ref[:]
    gsum = jnp.zeros((1, 128), F32)
    edges = None
    for b in range(blocks + 1):
        tall = 128 if b < blocks else 16
        conv = jnp.zeros((tall, 128), F32)
        adj = jnp.zeros((tall, 128), F32)
        for g in range(8):
            at = 1024 * b + tall * g
            conv = jnp.where(lane_group[:tall] == g, rf_ref[at : at + tall], conv)
            adj = jnp.where(lane_group[:tall] == g, ra_ref[at : at + tall], adj)
        at = slice(128 * b, 128 * b + 128)
        if b < blocks:
            query, key, value = (post[at].astype(F32) for post in posts)
            product = x_own[at].astype(F32)
            grad = cot_ref[at].astype(F32)
        else:
            query, key, value = after
            product = x_next.astype(F32)
            grad = cot_next
        direct = conv + skip * product
        gated = grad * query
        back = adj + skip * gated
        made = [(grad * direct).astype(BF), (back * value).astype(BF), (back * key).astype(BF)]
        if b < blocks:
            mixer_ref[at] = (query * direct).astype(BF)
            gsum = gsum + jnp.sum(gated * product, axis=0, keepdims=True)
            for a in range(parts):
                bp_ref[a, at] = made[a].astype(F32)
        else:
            edges = [m.astype(F32) for m in made]
    piece_ref[3, 0, 1:2] = gsum
    total = total_ref[...]
    for a in range(parts):
        post = bp_ref[a]
        edge0, edge1 = edges[a][0:1], edges[a][1:2]
        post1, post2 = post * mask1, post * mask2
        up1 = jnp.where(row == rows - 1, edge0 * next1[0:1], pltpu.roll(post1, rows - 1, 0))
        up2 = jnp.where(
            row == rows - 2,
            edge0 * next2[0:1],
            jnp.where(row == rows - 1, edge1 * next2[1:2], pltpu.roll(post2, rows - 2, 0)),
        )
        back_pre = (tap(0, a) * post + tap(1, a) * up1 + tap(2, a) * up2).astype(BF)
        pre = pre_ref[a, :].astype(F32)
        one, two = shifted_down(pre, pedge[2 * a : 2 * a + 1], pedge[2 * a + 1 : 2 * a + 2])
        sums = (
            jnp.sum(post * pre, axis=0, keepdims=True),
            jnp.sum(post1 * one, axis=0, keepdims=True),
            jnp.sum(post2 * two, axis=0, keepdims=True),
        )
        for t, value in enumerate(sums):
            k = t * parts + a
            if k < 8:
                piece_ref[2, 0, 16 + k : 17 + k] = value
            else:
                piece_ref[3, 0, 0:1] = value
        up_grad = dot(low, back_pre)
        if a == 0:
            piece_ref[0, 0, 16:24] = up_grad[:8]
            piece_ref[1, 0, :8] = up_grad[8:]
        elif a == 1:
            piece_ref[1, 0, 8:24] = up_grad
        else:
            piece_ref[2, 0, :16] = up_grad
        total = total + dot(up_ref[a, :], back_pre, 1, 1)
    total_ref[...] = total


    @pl.when(step == pl.num_programs(0) - 1)
    def _():
        for t in range(backlow_ref.shape[0]):
            backlow_ref[t] = total


def gather_kernel(lows_ref, got_ref, place_ref, sums_ref, out_ref):
    shards, cap, chans = got_ref.shape
    total = lows_ref[0]
    for t in range(1, lows_ref.shape[0]):
        total = total + lows_ref[t]
    placed = dot(total.astype(BF), place_ref[...]).astype(BF)
    down = jnp.concatenate(
        [
            dot(placed, got_ref[:, :, c : c + 256].reshape(shards * cap, 256))
            for c in range(0, chans, 256)
        ],
        1,
    )
    tiles = chans // 128
    for i in range(tiles):
        first = jnp.concatenate([down[:, 128 * i : 128 * i + 128], sums_ref[0, i, 16:]])
        out_ref[i] = first.astype(BF)
        for k in range(1, 4):
            out_ref[k * tiles + i] = sums_ref[k, i].astype(BF)


def sum_kernel(in_ref, out_ref):
    total = in_ref[0].astype(F32)
    for t in range(1, in_ref.shape[0]):
        total = total + in_ref[t].astype(F32)
    total = total.astype(BF)
    for t in range(out_ref.shape[0]):
        out_ref[t] = total


def spread_kernel(in_ref, down_ref, up_ref, short_ref, long_ref, gskip_ref):
    tiles = down_ref.shape[1] // 128
    flip = jnp.where(iota((128, 128), 0) + iota((128, 128), 1) == 127, 1.0, 0.0).astype(BF)
    for i in range(tiles):
        cols = slice(128 * i, 128 * i + 128)
        part = [in_ref[k * tiles + i].astype(F32) for k in range(4)]
        down_ref[:, cols] = part[0][:16]
        up_ref[0, :8, cols] = part[0][16:]
        up_ref[0, 8:, cols] = part[1][:8]
        up_ref[1, :, cols] = part[1][8:]
        up_ref[2, :, cols] = part[2][:16]
        short_ref[:8, cols] = part[2][16:]
        short_ref[8:9, cols] = part[3][0:1]
        gskip_ref[i : i + 1] = part[3][1:2]
        long_ref[8 * i : 8 * i + 8] = dot(part[3][8:16].astype(BF), flip)


def swap(value, axis):
    return lax.all_to_all(value, axis, split_axis=0, concat_axis=0, tiled=True)


def neighbour(value, steps):
    count = lax.axis_size("ctx")
    pairs = [(i, i + steps) for i in range(count) if 0 <= i + steps < count]
    return lax.ppermute(value, "ctx", pairs)


def doc_offsets(positions, lengths):
    index = jnp.arange(lengths.shape[0], dtype=I32)
    starts = jnp.sum(jnp.where(index[None, :] < index[:, None], lengths[None, :], 0), axis=1)
    begins = jnp.max(jnp.where(starts[None, :] <= positions[:, None], starts[None, :], 0), axis=1)
    return positions - begins


def on_device(
    tokens,
    frozen,
    cotangent,
    adapter_down_weight,
    adapter_up_weight,
    short_depthwise_filter,
    long_group_filter,
    skip_direct_scale,
    document_lengths,
    window_row_position,
):
    rows, chans = tokens.shape
    parts = frozen.shape[1]
    rank_dim = adapter_down_weight.shape[0]
    taps = short_depthwise_filter.shape[0]
    groups = long_group_filter.shape[0]
    shards = lax.axis_size("ctx")
    columns = lax.axis_size("tp")
    cap = 2 * rows // shards
    slots = shards * cap
    frozen = frozen.transpose(1, 0, 2)
    up = adapter_up_weight.transpose(1, 0, 2)
    pos_row = window_row_position.reshape(1, rows)
    vmem, far = pl.BlockSpec(memory_space=pltpu.VMEM), pl.BlockSpec(memory_space=pltpu.HBM)
    send, sel = pl.pallas_call(
        send_kernel,
        out_shape=(
            jax.ShapeDtypeStruct((shards, cap, parts * chans + 128), BF),
            jax.ShapeDtypeStruct((slots, rows), BF),
        ),
        in_specs=[vmem, far, far, vmem],
        out_specs=(far, vmem),
        scratch_shapes=[
            pltpu.VMEM((parts, rows, chans), BF),
            pltpu.VMEM((rows, chans), BF),
            pltpu.VMEM((parts, shards, cap, chans), BF),
            pltpu.VMEM((shards, cap, 128), BF),
            pltpu.SemaphoreType.DMA((parts + 1,)),
            pltpu.SemaphoreType.DMA((parts + 1,)),
        ],
        compiler_params=pltpu.CompilerParams(vmem_limit_bytes=66_000_000),
        cost_estimate=pl.CostEstimate(flops=1 << 30, bytes_accessed=5 << 20, transcendentals=0),
    )(pos_row, frozen, tokens, adapter_down_weight)
    got = swap(send, "ctx")

    send, sel, document_lengths, short_depthwise_filter = lax.optimization_barrier(
        (send, sel, document_lengths, short_depthwise_filter)
    )
    (send_tok,) = whole(
        send_tokens_kernel, [((shards, cap, chans), BF)], flops=2 * slots * rows * chans, nbytes=2 << 20
    )(sel, tokens)
    first = lax.axis_index("ctx") * rows
    offsets = doc_offsets(first + jnp.arange(rows + 256, dtype=I32), document_lengths).astype(F32)
    off_row = offsets.reshape(1, rows + 256)
    off_col = jnp.broadcast_to(offsets[:, None], (rows + 256, 128))
    tap_rows = short_depthwise_filter.reshape(taps * parts, chans).astype(F32)
    tap_rows = jnp.pad(tap_rows, ((0, 16 - taps * parts), (0, 0)))
    skip_row = skip_direct_scale.reshape(1, chans)
    got, send_tok, off_row, off_col, tap_rows = lax.optimization_barrier(
        (got, send_tok, off_row, off_col, tap_rows)
    )

    place, low_parts = tiled(
        place_kernel,
        1,
        [((shards, cap, 128), lambda i: (0, 0, parts * chans // 128))],
        [
            ((rows, slots), BF, (rows, slots), fixed2),
            ((columns, rank_dim, rows), F32, (columns, rank_dim, rows), lambda i: (0, 0, 0)),
        ],
        [],
        1 << 26,
        1 << 19,
        60_000_000,
    )(got)
    lows = swap(low_parts, "tp")
    got, lows = lax.optimization_barrier((got, lows))
    wide = 256
    steps = chans // wide
    pre, post, x, back, ahead, behind, low = tiled(
        post_kernel,
        steps,
        [((shards, cap, wide), lambda i, a=a: (0, 0, a * steps + i)) for a in range(parts)]
        + [
            ((rows, slots), fixed2),
            ((columns, rank_dim, rows), lambda i: (0, 0, 0)),
            ((parts, rank_dim, wide), at3),
            ((16, wide), at2),
            ((rows + 256, 128), fixed2),
            ((rows, wide), at2),
        ],
        [
            ((parts, rows, chans), BF, (parts, rows, wide), at3),
            ((parts, rows, chans), BF, (parts, rows, wide), at3),
            ((rows, chans), BF, (rows, wide), at2),
            ((rows, chans), BF, (rows, wide), at2),
            ((144, chans), BF, (144, wide), at2),
            ((144, chans), BF, (144, wide), at2),
            ((rank_dim, rows), BF, (rank_dim, rows), fixed2),
        ],
        [
            pltpu.VMEM((16, wide), F32),
            pltpu.VMEM((16, wide), F32),
            pltpu.VMEM((rows, rank_dim), BF),
        ],
        1 << 30,
        8 << 20,
        60_000_000,
    )(got, got, got, place, lows, up, tap_rows, off_col, cotangent)
    send_tok, ahead, behind = lax.optimization_barrier((send_tok, ahead, behind))
    from_prev = neighbour(ahead, 1)
    from_next = neighbour(behind, -1)
    got_tok = swap(send_tok, "ctx")
    blocks = rows // 128
    tall = 1024 * blocks + 128
    mixer, sums, back_low_part = tiled(
        main_kernel,
        chans // 128,
        [
            ((parts, rows, 128), at3),
            ((parts, rows, 128), at3),
            ((rows, 128), at2),
            ((rows, 128), at2),
            ((144, 128), at2),
            ((144, 128), at2),
            ((rows, 128), at2),
            ((16, 128), at2),
            ((1, 128), at2),
            ((8, 128), lambda i: (i, 0)),
            ((rows + 256, 128), fixed2),
            ((1, rows + 256), fixed2),
            ((rank_dim, rows), fixed2),
            ((parts, rank_dim, 128), at3),
        ],
        [
            ((rows, chans), BF, (rows, 128), at2),
            ((4, chans // 128, 24, 128), F32, (4, 1, 24, 128), lambda i: (0, i, 0, 0)),
            ((columns, rank_dim, rows), F32, (columns, rank_dim, rows), lambda i: (0, 0, 0)),
        ],
        [
            pltpu.VMEM((128 * blocks + 16, 256), BF),
            pltpu.VMEM((128 * blocks + 16, 256), BF),
            pltpu.VMEM((blocks, 128, 256), F32),
            pltpu.VMEM((8, 128), F32),
            pltpu.VMEM((8, 128), F32),
            pltpu.VMEM((tall, 256), BF),
            pltpu.VMEM((tall, 256), BF),
            pltpu.VMEM((1024, 128), BF),
            pltpu.VMEM((tall, 128), F32),
            pltpu.VMEM((tall, 128), F32),
            pltpu.VMEM((blocks, 1024, 256), F32),
            pltpu.VMEM((parts, rows, 128), F32),
            pltpu.VMEM((rank_dim, rows), F32),
        ],
        10 << 30,
        8 << 20,
        60_000_000,
    )(pre, post, x, back, from_prev, from_next, cotangent, tap_rows, skip_row, long_group_filter,
      off_col, off_row, low, up)
    got_tok, back_low_part = lax.optimization_barrier((got_tok, back_low_part))
    back_lows = swap(back_low_part, "tp")
    (pieces,) = whole(
        gather_kernel, [((shards, 24, 128), BF)], flops=1 << 26, nbytes=2 << 20
    )(back_lows, got_tok, place, sums)
    pieces = swap(pieces, "ctx")
    (pieces,) = whole(sum_kernel, [((shards, 24, 128), BF)], flops=1 << 20, nbytes=1 << 20)(pieces)
    pieces = swap(pieces, "ctx")
    grad_down, up_gradient, grad_short, grad_long, grad_skip = whole(
        spread_kernel,
        [
            ((rank_dim, chans), F32),
            ((parts, rank_dim, chans), F32),
            ((taps * parts, chans), F32),
            ((groups, 128), F32),
            ((chans // 128, 128), F32),
        ],
        flops=1 << 20,
        nbytes=1 << 20,
    )(pieces)
    return (
        mixer,
        grad_down,
        up_gradient.transpose(1, 0, 2),
        grad_short.reshape(taps, parts, chans),
        grad_long,
        grad_skip.reshape(chans),
    )


def solution(mesh):
    placed = (
        P("ctx", "tp"),
        P("ctx", None, "tp"),
        P("ctx", "tp"),
        P(None, "tp"),
        P(None, None, "tp"),
        P(None, None, "tp"),
        P("tp", None),
        P("tp"),
        P(),
        P("ctx"),
    )
    return jax.shard_map(
        on_device,
        mesh=mesh,
        in_specs=placed,
        out_specs=(
            P("ctx", "tp"),
            P(None, "tp"),
            P(None, None, "tp"),
            P(None, None, "tp"),
            P("tp", None),
            P("tp"),
        ),
        check_vma=False,
    )
```

```python
import functools

import jax
import jax.numpy as jnp
from jax import lax
from jax.experimental import pallas as pl
from jax.experimental.pallas import tpu as pltpu
from jax.sharding import PartitionSpec as P

BF = jnp.bfloat16
F32 = jnp.float32
I32 = jnp.int32


def whole(kernel, outs, scratch=(), flops=0, nbytes=0):
    def call(*args):
        return pl.pallas_call(
            kernel,
            out_shape=tuple(jax.ShapeDtypeStruct(s, d) for s, d in outs),
            in_specs=[pl.BlockSpec(memory_space=pltpu.VMEM)] * len(args),
            out_specs=tuple(pl.BlockSpec(memory_space=pltpu.VMEM) for _ in outs),
            scratch_shapes=list(scratch),
            compiler_params=pltpu.CompilerParams(vmem_limit_bytes=20 << 20),
            cost_estimate=pl.CostEstimate(flops=flops, bytes_accessed=nbytes, transcendentals=0),
        )(*args)

    return call


def tiled(kernel, grid, in_specs, outs, scratch, flops, nbytes, limit):
    def call(*args):
        return pl.pallas_call(
            kernel,
            grid=(grid,),
            out_shape=tuple(jax.ShapeDtypeStruct(s, d) for s, d, _, _ in outs),
            in_specs=[pl.BlockSpec(b, m) for b, m in in_specs],
            out_specs=tuple(pl.BlockSpec(b, m) for _, _, b, m in outs),
            scratch_shapes=list(scratch),
            compiler_params=pltpu.CompilerParams(
                vmem_limit_bytes=limit, dimension_semantics=("arbitrary",)
            ),
            cost_estimate=pl.CostEstimate(flops=flops, bytes_accessed=nbytes, transcendentals=0),
        )(*args)

    return call


def at2(i):
    return (0, i)


def at3(i):
    return (0, 0, i)


def fixed2(i):
    return (0, 0)


def dot(a, b, ca=1, cb=0):
    return lax.dot_general(a, b, (((ca,), (cb,)), ((), ())), preferred_element_type=F32)


def iota(shape, dim):
    return lax.broadcasted_iota(I32, shape, dim)


def send_kernel(pos_ref, frozen_ref, out_ref, sel_ref, in_buf, out_buf, in_sem, out_sem):
    rows = pos_ref.shape[1]
    slots = sel_ref.shape[0]
    parts, shards, cap, chans = out_buf.shape
    loads = [
        pltpu.make_async_copy(frozen_ref.at[a], in_buf.at[a], in_sem.at[a]) for a in range(parts)
    ]
    for load in loads:
        load.start()
    dest = (pos_ref[...] // rows).astype(F32)
    dest_row = jnp.broadcast_to(dest, (rows, rows))
    dest_col = dest_row.T
    earlier = (dest_row == dest_col) & (iota((rows, rows), 0) < iota((rows, rows), 1))
    rank = jnp.sum(jnp.where(earlier, 1.0, 0.0), axis=0, keepdims=True)
    slot = dest * float(cap) + rank
    sel = jnp.where(
        iota((slots, rows), 0).astype(F32) == jnp.broadcast_to(slot, (slots, rows)), 1.0, 0.0
    ).astype(BF)
    sel_ref[...] = sel
    stores = []
    for a in range(parts):
        loads[a].wait()
        for c in range(0, chans, 256):
            out_buf[a, :, :, c : c + 256] = (
                dot(sel, in_buf[a, :, c : c + 256]).astype(BF).reshape(shards, cap, 256)
            )
        store = pltpu.make_async_copy(
            out_buf.at[a], out_ref.at[:, :, pl.ds(a * chans, chans)], out_sem.at[a]
        )
        store.start()
        stores.append(store)
    for store in stores:
        store.wait()


def low_kernel(tok_ref, down_ref, out_ref):
    out_ref[...] = dot(down_ref[...], tok_ref[...], 1, 1)


def send_tokens_kernel(sel_ref, tok_ref, out_ref):
    shards, cap, chans = out_ref.shape
    for c in range(0, chans, 256):
        out_ref[:, :, c : c + 256] = (
            dot(sel_ref[...], tok_ref[:, c : c + 256]).astype(BF).reshape(shards, cap, 256)
        )


def place_kernel(cap, all_ref, shard_ref, place_ref, low_ref):
    rows, slots = place_ref.shape
    rank_dim = low_ref.shape[0]
    group = 128 // cap
    row, col = iota((rows, rows), 0), iota((rows, rows), 1)
    before = jnp.where(row < col, 1.0, 0.0).astype(BF)
    shard = shard_ref[0:1, 0:1]
    low = jnp.zeros((rank_dim, rows), F32)
    for j in range(slots // 128):
        total = jnp.zeros((rows, 128), F32)
        for k in range(group):
            at = (j * group + k) * rows
            block = all_ref[:, at : at + rows]
            where = block[rank_dim : rank_dim + 8].astype(F32)
            hit = jnp.where(where == shard, 1.0, 0.0)[0:1]
            rank = dot(jnp.broadcast_to(hit, (16, rows)).astype(BF), before)[0:1]
            target = where[1:2] * hit - (1.0 - hit)
            sel = jnp.where(jnp.broadcast_to(target, (rows, rows)) == row.astype(F32), 1.0, 0.0)
            sel = sel.astype(BF)
            slot = rank + float(cap * k)
            into = jnp.where(
                jnp.broadcast_to(slot, (128, rows)) == iota((128, rows), 0).astype(F32), hit, 0.0
            )
            total = total + dot(sel, into.astype(BF), 1, 1)
            low = low + dot(block[:rank_dim], sel, 1, 1)
        place_ref[:, 128 * j : 128 * j + 128] = total.astype(BF)
    low_ref[...] = low.astype(BF)


def shifted_down(value, edge0, edge1):
    row = iota(value.shape, 0)
    one = jnp.where(row == 0, edge1, pltpu.roll(value, 1, 0))
    two = jnp.where(row == 0, edge0, jnp.where(row == 1, edge1, pltpu.roll(value, 2, 0)))
    return one, two


def post_kernel(
    got0_ref, got1_ref, got2_ref, place_ref, low_ref, up_ref, taps_ref, offr_ref, cot_ref,
    pre_ref, post_ref, x_ref, b_ref, ahead_ref, behind_ref,
    ahead_edge, behind_edge, low_t_ref, mask_ref,
):
    parts, rows, width = pre_ref.shape
    slots = place_ref.shape[1]

    @pl.when(pl.program_id(0) == 0)
    def _():
        low_t_ref[...] = low_ref[...].astype(F32).T.astype(BF)
        for b in range(rows // 128):
            off = columns_of(offr_ref[:, 128 * b : 128 * b + 128])
            mask_ref[0, 128 * b : 128 * b + 128] = jnp.where(off >= 1.0, 1.0, 0.0)
            mask_ref[1, 128 * b : 128 * b + 128] = jnp.where(off >= 2.0, 1.0, 0.0)

    mask1 = jnp.concatenate([mask_ref[0]] * (width // 128), 1)
    mask2 = jnp.concatenate([mask_ref[1]] * (width // 128), 1)
    ahead_edge[...] = jnp.zeros_like(ahead_edge)
    behind_edge[...] = jnp.zeros_like(behind_edge)
    nothing = jnp.zeros((1, width), F32)
    made = []
    for a, got_ref in enumerate((got0_ref, got1_ref, got2_ref)):
        value = dot(place_ref[...], got_ref[...].reshape(slots, width)) + dot(low_t_ref[...], up_ref[a])
        value = value.astype(BF)
        pre_ref[a] = value
        value = value.astype(F32)
        ahead_edge[2 * a : 2 * a + 2] = value[rows - 2 :]
        behind_edge[2 * a : 2 * a + 2] = value[:2]
        one, two = shifted_down(value, nothing, nothing)
        total = (
            taps_ref[a : a + 1] * value
            + taps_ref[parts + a : parts + a + 1] * one * mask1
            + taps_ref[2 * parts + a : 2 * parts + a + 1] * two * mask2
        ).astype(BF)
        post_ref[a] = total
        made.append(total.astype(F32))
    product = (made[1] * made[2]).astype(BF)
    grad = cot_ref[...].astype(F32)
    back = (grad * made[0]).astype(BF)
    x_ref[...] = product
    b_ref[...] = back
    ahead_ref[:128] = product[rows - 128 :]
    behind_ref[:128] = back[:128]
    behind_edge[6:8] = grad[:2]
    behind_edge[8:9] = back[128:144].astype(F32)[:1]
    ahead_ref[128:] = ahead_edge[...].astype(BF)
    behind_ref[128:] = behind_edge[...].astype(BF)


def columns_of(row):
    return jnp.broadcast_to(row, (128, row.shape[1])).T


def bank_kernel(filt_ref, offr_ref, fwd_ref, adj_ref, mfwd_ref, madj_ref, frow_ref, grow_ref):
    blocks = offr_ref.shape[1] // 128 - 2
    sub, lane = iota((128, 128), 0), iota((128, 128), 1)

    @pl.when(pl.program_id(0) == 0)
    def _():
        for b in range(blocks + 1):
            first = 128 * b
            tall = 128 if b < blocks else 16
            prev, own = forward_masks(offr_ref, first)
            mfwd_ref[first : first + tall, :128] = prev.astype(BF)[:tall]
            mfwd_ref[first : first + tall, 128:] = own.astype(BF)[:tall]
            begin0 = (first + lane).astype(F32) - offr_ref[:, first : first + 128]
            begin1 = (first + 128 + lane).astype(F32) - offr_ref[:, first + 128 : first + 256]
            at = (first + sub).astype(F32)
            same = jnp.where((sub <= lane) & (at >= begin0), 1.0, 0.0).astype(BF)
            after = jnp.where((lane < sub) & (at >= begin1), 1.0, 0.0).astype(BF)
            madj_ref[first : first + tall, :128] = same[:tall]
            madj_ref[first : first + tall, 128:] = after[:tall]

    filt = filt_ref[...]
    flip = jnp.where((sub + lane) % 128 == 0, 1.0, 0.0).astype(BF)
    frow_ref[...] = filt.astype(F32)
    grow_ref[...] = dot(filt, flip)
    for g in range(8):
        f_row = jnp.broadcast_to(frow_ref[g : g + 1, :], (128, 128))
        g_row = jnp.broadcast_to(grow_ref[g : g + 1, :], (128, 128))
        circ = pltpu.roll(f_row, 0, 1, stride=1, stride_axis=0).astype(BF)
        circ_t = pltpu.roll(g_row, 0, 1, stride=1, stride_axis=0).astype(BF)
        two, two_t = jnp.concatenate([circ, circ], 1), jnp.concatenate([circ_t, circ_t], 1)
        for b in range(blocks + 1):
            tall = 128 if b < blocks else 16
            at = 1024 * b + tall * g
            fwd_ref[0, at : at + tall] = two_t[:tall] * mfwd_ref[128 * b : 128 * b + tall]
            adj_ref[0, at : at + tall] = two[:tall] * madj_ref[128 * b : 128 * b + tall]


def forward_masks(offr_ref, first):
    sub, lane = iota((128, 128), 0), iota((128, 128), 1)
    begin = (first + sub).astype(F32) - columns_of(offr_ref[:, first : first + 128])
    own = (lane <= sub) & ((first + lane).astype(F32) >= begin)
    prev = (lane > sub) & ((first - 128 + lane).astype(F32) >= begin)
    return jnp.where(prev, 1.0, 0.0), jnp.where(own, 1.0, 0.0)


def main_kernel(
    pre_ref, post_ref, x_ref, b_ref, prev_ref, next_ref, cot_ref, taps_ref, skip_ref, fwd_ref, adj_ref,
    offr_ref, low_ref, up_ref,
    mixer_ref, piece_ref, backlow_ref,
    mpair_ref, mask_ref, lhs_ref, rf_ref, ra_ref, rp_ref, bp_ref, total_ref,
):
    parts, rows, _ = pre_ref.shape
    step = pl.program_id(0)
    rank_dim = low_ref.shape[0]
    blocks = rows // 128
    sub, lane = iota((128, 128), 0), iota((128, 128), 1)
    turn = jnp.where(sub + lane == 127, 1.0, 0.0).astype(BF)

    @pl.when(step == 0)
    def _():
        total_ref[...] = jnp.zeros_like(total_ref)
        for b in range(blocks):
            prev, own = forward_masks(offr_ref, 128 * b)
            mpair_ref[b, :, :128] = dot(turn, prev.astype(BF))
            mpair_ref[b, :, 128:] = dot(turn, own.astype(BF))
        for b in range(blocks + 1):
            off = columns_of(offr_ref[:, 128 * b : 128 * b + 128])
            mask_ref[0, 128 * b : 128 * b + 128] = jnp.where(off >= 1.0, 1.0, 0.0)
            mask_ref[1, 128 * b : 128 * b + 128] = jnp.where(off >= 2.0, 1.0, 0.0)

    mask1, mask2 = mask_ref[0, :rows], mask_ref[1, :rows]
    next1, next2 = mask_ref[0, rows : rows + 16], mask_ref[1, rows : rows + 16]
    low = low_ref[...]
    row = iota((rows, 128), 0)
    top = iota((16, 128), 0) < 2
    lane_group = lane // 16
    piece_ref[...] = jnp.zeros_like(piece_ref)

    def tap(s, a):
        return taps_ref[s * parts + a : s * parts + a + 1]

    pedge = prev_ref[128:].astype(F32)
    nedge = next_ref[128:].astype(F32)
    heads, after = [], []
    for a in range(parts):
        head = pre_ref[a, :16].astype(F32)
        one, two = shifted_down(head, pedge[2 * a : 2 * a + 1], pedge[2 * a + 1 : 2 * a + 2])
        heads.append(
            (tap(0, a) * head + tap(1, a) * one * mask1[:16] + tap(2, a) * two * mask2[:16]).astype(BF)
        )
        tail = pre_ref[a, rows - 16 :].astype(F32)
        head = nedge if a == 0 else pltpu.roll(nedge, 16 - 2 * a, 0)
        one, two = shifted_down(head, tail[14:15], tail[15:16])
        after.append(
            (tap(0, a) * head + tap(1, a) * one * next1 + tap(2, a) * two * next2)
            .astype(BF)
            .astype(F32)
        )
    posts = [jnp.concatenate([heads[a], post_ref[a, 16:]]) for a in range(parts)]
    x_head = (heads[1].astype(F32) * heads[2].astype(F32)).astype(BF)
    b_head = (cot_ref[:16].astype(F32) * heads[0].astype(F32)).astype(BF)
    x_next = jnp.where(top, after[1] * after[2], 0.0).astype(BF)
    cot_next = pltpu.roll(nedge, 10, 0)
    b_next = jnp.where(top, cot_next * after[0], next_ref[:16].astype(F32)).astype(BF)
    b_last = jnp.where(iota((16, 128), 0) == 0, pltpu.roll(nedge, 8, 0), 0.0).astype(BF)
    blank = jnp.zeros((112, 128), BF)
    x_own = jnp.concatenate([x_head, x_ref[16:]])
    x_win = jnp.concatenate([prev_ref[:128], x_own, x_next, blank])
    b_win = jnp.concatenate(
        [b_head, b_ref[16:], b_next, next_ref[16:128], b_last, blank]
    )
    for b in range(blocks + 1):
        at = slice(1024 * b, 1024 * b + (1024 if b < blocks else 128))
        xw = x_win[128 * b : 128 * b + 256]
        rf_ref[at] = dot(fwd_ref[0, at], xw)
        ra_ref[at] = dot(adj_ref[0, at], b_win[128 * b : 128 * b + 256])
    backs = [dot(turn, b_win[128 * b : 128 * b + 128]) for b in range(blocks)]
    for g in range(8):
        part = jnp.zeros((128, 128), F32)
        for b in range(blocks):
            lhs = jnp.where(lane_group == g, backs[b], 0.0).astype(BF)
            pair = dot(lhs, x_win[128 * b : 128 * b + 256], 1, 1) * mpair_ref[b]
            part = part + pair[:, :128] + pair[:, 128:]
        part = pltpu.roll(part, 0, 1, stride=1, stride_axis=0)
        piece_ref[3, 0, 8 + g : 9 + g] = jnp.sum(part, axis=0, keepdims=True)
    skip = skip_ref[:]
    gsum = jnp.zeros((1, 128), F32)
    edges = None
    for b in range(blocks + 1):
        tall = 128 if b < blocks else 16
        conv = jnp.zeros((tall, 128), F32)
        adj = jnp.zeros((tall, 128), F32)
        for g in range(8):
            at = 1024 * b + tall * g
            conv = jnp.where(lane_group[:tall] == g, rf_ref[at : at + tall], conv)
            adj = jnp.where(lane_group[:tall] == g, ra_ref[at : at + tall], adj)
        at = slice(128 * b, 128 * b + 128)
        if b < blocks:
            query, key, value = (post[at].astype(F32) for post in posts)
            product = x_own[at].astype(F32)
            grad = cot_ref[at].astype(F32)
        else:
            query, key, value = after
            product = x_next.astype(F32)
            grad = cot_next
        direct = conv + skip * product
        gated = grad * query
        back = adj + skip * gated
        made = [(grad * direct).astype(BF), (back * value).astype(BF), (back * key).astype(BF)]
        if b < blocks:
            mixer_ref[at] = (query * direct).astype(BF)
            gsum = gsum + jnp.sum(gated * product, axis=0, keepdims=True)
            for a in range(parts):
                bp_ref[a, at] = made[a].astype(F32)
        else:
            edges = [m.astype(F32) for m in made]
    piece_ref[3, 0, 1:2] = gsum
    total = total_ref[...]
    for a in range(parts):
        post = bp_ref[a]
        edge0, edge1 = edges[a][0:1], edges[a][1:2]
        post1, post2 = post * mask1, post * mask2
        up1 = jnp.where(row == rows - 1, edge0 * next1[0:1], pltpu.roll(post1, rows - 1, 0))
        up2 = jnp.where(
            row == rows - 2,
            edge0 * next2[0:1],
            jnp.where(row == rows - 1, edge1 * next2[1:2], pltpu.roll(post2, rows - 2, 0)),
        )
        back_pre = (tap(0, a) * post + tap(1, a) * up1 + tap(2, a) * up2).astype(BF)
        pre = pre_ref[a, :].astype(F32)
        one, two = shifted_down(pre, pedge[2 * a : 2 * a + 1], pedge[2 * a + 1 : 2 * a + 2])
        sums = (
            jnp.sum(post * pre, axis=0, keepdims=True),
            jnp.sum(post1 * one, axis=0, keepdims=True),
            jnp.sum(post2 * two, axis=0, keepdims=True),
        )
        for t, value in enumerate(sums):
            k = t * parts + a
            if k < 8:
                piece_ref[2, 0, 16 + k : 17 + k] = value
            else:
                piece_ref[3, 0, 0:1] = value
        up_grad = dot(low, back_pre)
        if a == 0:
            piece_ref[0, 0, 16:24] = up_grad[:8]
            piece_ref[1, 0, :8] = up_grad[8:]
        elif a == 1:
            piece_ref[1, 0, 8:24] = up_grad
        else:
            piece_ref[2, 0, :16] = up_grad
        total = total + dot(up_ref[a, :], back_pre, 1, 1)
    total_ref[...] = total


    @pl.when(step == pl.num_programs(0) - 1)
    def _():
        for t in range(backlow_ref.shape[0]):
            backlow_ref[t] = total


def gather_kernel(lows_ref, got_ref, place_ref, sums_ref, out_ref):
    shards, cap, chans = got_ref.shape
    total = lows_ref[0]
    for t in range(1, lows_ref.shape[0]):
        total = total + lows_ref[t]
    placed = dot(total.astype(BF), place_ref[...]).astype(BF)
    down = jnp.concatenate(
        [
            dot(placed, got_ref[:, :, c : c + 256].reshape(shards * cap, 256))
            for c in range(0, chans, 256)
        ],
        1,
    )
    tiles = chans // 128
    for i in range(tiles):
        first = jnp.concatenate([down[:, 128 * i : 128 * i + 128], sums_ref[0, i, 16:]])
        out_ref[i] = first.astype(BF)
        for k in range(1, 4):
            out_ref[k * tiles + i] = sums_ref[k, i].astype(BF)


def sum_kernel(in_ref, out_ref):
    total = in_ref[0].astype(F32)
    for t in range(1, in_ref.shape[0]):
        total = total + in_ref[t].astype(F32)
    total = total.astype(BF)
    for t in range(out_ref.shape[0]):
        out_ref[t] = total


def spread_kernel(in_ref, down_ref, up_ref, short_ref, long_ref, gskip_ref):
    tiles = down_ref.shape[1] // 128
    flip = jnp.where(iota((128, 128), 0) + iota((128, 128), 1) == 127, 1.0, 0.0).astype(BF)
    for i in range(tiles):
        cols = slice(128 * i, 128 * i + 128)
        part = [in_ref[k * tiles + i].astype(F32) for k in range(4)]
        down_ref[:, cols] = part[0][:16]
        up_ref[0, :8, cols] = part[0][16:]
        up_ref[0, 8:, cols] = part[1][:8]
        up_ref[1, :, cols] = part[1][8:]
        up_ref[2, :, cols] = part[2][:16]
        for k in range(9):
            row = part[2][16 + k : 17 + k] if k < 8 else part[3][0:1]
            short_ref[k // 3, k % 3 : k % 3 + 1, cols] = row
        gskip_ref[i : i + 1] = part[3][1:2]
        long_ref[8 * i : 8 * i + 8] = dot(part[3][8:16].astype(BF), flip)


def swap(value, axis):
    return lax.all_to_all(value, axis, split_axis=0, concat_axis=0, tiled=True)


def neighbour(value, steps):
    count = lax.axis_size("ctx")
    pairs = [(i, i + steps) for i in range(count) if 0 <= i + steps < count]
    return lax.ppermute(value, "ctx", pairs)


def partner(value, axis, bit):
    return lax.ppermute(value, axis, [(i, i ^ bit) for i in range(lax.axis_size(axis))])


def doc_offsets(positions, lengths):
    index = jnp.arange(lengths.shape[0], dtype=I32)
    starts = jnp.sum(jnp.where(index[None, :] < index[:, None], lengths[None, :], 0), axis=1)
    begins = jnp.max(jnp.where(starts[None, :] <= positions[:, None], starts[None, :], 0), axis=1)
    return positions - begins


def on_device(
    tokens,
    frozen,
    cotangent,
    adapter_down_weight,
    adapter_up_weight,
    short_depthwise_filter,
    long_group_filter,
    skip_direct_scale,
    document_lengths,
    window_row_position,
):
    rows, chans = tokens.shape
    parts = frozen.shape[1]
    rank_dim = adapter_down_weight.shape[0]
    taps = short_depthwise_filter.shape[0]
    groups = long_group_filter.shape[0]
    shards = lax.axis_size("ctx")
    columns = lax.axis_size("tp")
    cap = 2 * rows // shards
    slots = shards * cap
    frozen = frozen.transpose(1, 0, 2)
    up = adapter_up_weight.transpose(1, 0, 2)
    pos_row = window_row_position.reshape(1, rows)
    vmem, far = pl.BlockSpec(memory_space=pltpu.VMEM), pl.BlockSpec(memory_space=pltpu.HBM)
    send, sel = pl.pallas_call(
        send_kernel,
        out_shape=(
            jax.ShapeDtypeStruct((shards, cap, parts * chans), BF),
            jax.ShapeDtypeStruct((slots, rows), BF),
        ),
        in_specs=[vmem, far],
        out_specs=(far, vmem),
        scratch_shapes=[
            pltpu.VMEM((parts, rows, chans), BF),
            pltpu.VMEM((parts, shards, cap, chans), BF),
            pltpu.SemaphoreType.DMA((parts,)),
            pltpu.SemaphoreType.DMA((parts,)),
        ],
        compiler_params=pltpu.CompilerParams(vmem_limit_bytes=66_000_000),
        cost_estimate=pl.CostEstimate(flops=1 << 30, bytes_accessed=5 << 20, transcendentals=0),
    )(pos_row, frozen)
    got = swap(send, "ctx")

    send, sel, document_lengths, short_depthwise_filter, adapter_down_weight = lax.optimization_barrier(
        (send, sel, document_lengths, short_depthwise_filter, adapter_down_weight)
    )
    (low_sum,) = whole(low_kernel, [((rank_dim, rows), F32)], flops=1 << 23, nbytes=1 << 19)(
        tokens, adapter_down_weight
    )
    for bit in range(3):
        low_sum = low_sum + partner(low_sum, "tp", 1 << bit)
    where = jnp.concatenate([pos_row // rows, pos_row % rows]).astype(BF)
    packet = jnp.concatenate([low_sum.astype(BF), where, jnp.zeros((6, rows), BF)])
    packets = lax.all_gather(packet, "ctx", axis=1, tiled=True)
    shard = jnp.full((1, 128), lax.axis_index("ctx"), F32)
    place, low = whole(
        functools.partial(place_kernel, cap),
        [((rows, slots), BF), ((rank_dim, rows), BF)],
        flops=1 << 30,
        nbytes=1 << 20,
    )(packets, shard)
    (send_tok,) = whole(
        send_tokens_kernel, [((shards, cap, chans), BF)], flops=2 * slots * rows * chans, nbytes=2 << 20
    )(sel, tokens)
    first = lax.axis_index("ctx") * rows
    offsets = doc_offsets(first + jnp.arange(rows + 256, dtype=I32), document_lengths).astype(F32)
    off_row = offsets.reshape(1, rows + 256)
    tap_rows = short_depthwise_filter.reshape(taps * parts, chans).astype(F32)
    tap_rows = jnp.pad(tap_rows, ((0, 16 - taps * parts), (0, 0)))
    skip_row = skip_direct_scale.reshape(1, chans)
    blocks = rows // 128
    tall = 1024 * blocks + 128
    tiles = chans // 128
    fwd_bank, adj_bank = tiled(
        bank_kernel,
        tiles,
        [((8, 128), lambda i: (i, 0)), ((1, rows + 256), fixed2)],
        [((tiles, tall, 256), BF, (1, tall, 256), lambda i: (i, 0, 0))] * 2,
        [
            pltpu.VMEM((128 * blocks + 16, 256), BF),
            pltpu.VMEM((128 * blocks + 16, 256), BF),
            pltpu.VMEM((8, 128), F32),
            pltpu.VMEM((8, 128), F32),
        ],
        1 << 30,
        18 << 20,
        60_000_000,
    )(long_group_filter, off_row)
    got, send_tok, off_row, fwd_bank, adj_bank, tap_rows, place, low = lax.optimization_barrier(
        (got, send_tok, off_row, fwd_bank, adj_bank, tap_rows, place, low)
    )

    wide = 256
    steps = chans // wide
    pre, post, x, back, ahead, behind = tiled(
        post_kernel,
        steps,
        [((shards, cap, wide), lambda i, a=a: (0, 0, a * steps + i)) for a in range(parts)]
        + [
            ((rows, slots), fixed2),
            ((rank_dim, rows), fixed2),
            ((parts, rank_dim, wide), at3),
            ((16, wide), at2),
            ((1, rows + 256), fixed2),
            ((rows, wide), at2),
        ],
        [
            ((parts, rows, chans), BF, (parts, rows, wide), at3),
            ((parts, rows, chans), BF, (parts, rows, wide), at3),
            ((rows, chans), BF, (rows, wide), at2),
            ((rows, chans), BF, (rows, wide), at2),
            ((144, chans), BF, (144, wide), at2),
            ((144, chans), BF, (144, wide), at2),
        ],
        [
            pltpu.VMEM((16, wide), F32),
            pltpu.VMEM((16, wide), F32),
            pltpu.VMEM((rows, rank_dim), BF),
            pltpu.VMEM((2, rows, 128), F32),
        ],
        1 << 30,
        8 << 20,
        60_000_000,
    )(got, got, got, place, low, up, tap_rows, off_row, cotangent)
    send_tok, ahead, behind = lax.optimization_barrier((send_tok, ahead, behind))
    from_prev = neighbour(ahead, 1)
    from_next = neighbour(behind, -1)
    got_tok = swap(send_tok, "ctx")
    mixer, sums, back_low_part = tiled(
        main_kernel,
        chans // 128,
        [
            ((parts, rows, 128), at3),
            ((parts, rows, 128), at3),
            ((rows, 128), at2),
            ((rows, 128), at2),
            ((144, 128), at2),
            ((144, 128), at2),
            ((rows, 128), at2),
            ((16, 128), at2),
            ((1, 128), at2),
            ((1, tall, 256), lambda i: (i, 0, 0)),
            ((1, tall, 256), lambda i: (i, 0, 0)),
            ((1, rows + 256), fixed2),
            ((rank_dim, rows), fixed2),
            ((parts, rank_dim, 128), at3),
        ],
        [
            ((rows, chans), BF, (rows, 128), at2),
            ((4, chans // 128, 24, 128), F32, (4, 1, 24, 128), lambda i: (0, i, 0, 0)),
            ((columns, rank_dim, rows), F32, (columns, rank_dim, rows), lambda i: (0, 0, 0)),
        ],
        [
            pltpu.VMEM((blocks, 128, 256), F32),
            pltpu.VMEM((2, rows + 128, 128), F32),
            pltpu.VMEM((1024, 128), BF),
            pltpu.VMEM((tall, 128), F32),
            pltpu.VMEM((tall, 128), F32),
            pltpu.VMEM((blocks, 1024, 256), F32),
            pltpu.VMEM((parts, rows, 128), F32),
            pltpu.VMEM((rank_dim, rows), F32),
        ],
        10 << 30,
        8 << 20,
        60_000_000,
    )(pre, post, x, back, from_prev, from_next, cotangent, tap_rows, skip_row, fwd_bank, adj_bank,
      off_row, low, up)
    got_tok, back_low_part = lax.optimization_barrier((got_tok, back_low_part))
    back_lows = swap(back_low_part, "tp")
    (pieces,) = whole(
        gather_kernel, [((shards, 24, 128), BF)], flops=1 << 26, nbytes=2 << 20
    )(back_lows, got_tok, place, sums)
    pieces = swap(pieces, "ctx")
    (pieces,) = whole(sum_kernel, [((shards, 24, 128), BF)], flops=1 << 20, nbytes=1 << 20)(pieces)
    pieces = swap(pieces, "ctx")
    grad_down, up_gradient, grad_short, grad_long, grad_skip = whole(
        spread_kernel,
        [
            ((rank_dim, chans), F32),
            ((parts, rank_dim, chans), F32),
            ((taps, parts, chans), F32),
            ((groups, 128), F32),
            ((chans // 128, 128), F32),
        ],
        flops=1 << 20,
        nbytes=1 << 20,
    )(pieces)
    return (
        mixer,
        grad_down,
        up_gradient.transpose(1, 0, 2),
        grad_short,
        grad_long,
        grad_skip.reshape(chans),
    )


def solution(mesh):
    placed = (
        P("ctx", "tp"),
        P("ctx", None, "tp"),
        P("ctx", "tp"),
        P(None, "tp"),
        P(None, None, "tp"),
        P(None, None, "tp"),
        P("tp", None),
        P("tp"),
        P(),
        P("ctx"),
    )
    return jax.shard_map(
        on_device,
        mesh=mesh,
        in_specs=placed,
        out_specs=(
            P("ctx", "tp"),
            P(None, "tp"),
            P(None, None, "tp"),
            P(None, None, "tp"),
            P("tp", None),
            P("tp"),
        ),
        check_vma=False,
    )
```

```python
import jax
import jax.numpy as jnp
from jax import lax
from jax.experimental import pallas as pl
from jax.experimental.pallas import tpu as pltpu
from jax.sharding import PartitionSpec as P

BF = jnp.bfloat16
F32 = jnp.float32
I32 = jnp.int32


def whole(kernel, outs, scratch=(), flops=0, nbytes=0):
    def call(*args):
        return pl.pallas_call(
            kernel,
            out_shape=tuple(jax.ShapeDtypeStruct(s, d) for s, d in outs),
            in_specs=[pl.BlockSpec(memory_space=pltpu.VMEM)] * len(args),
            out_specs=tuple(pl.BlockSpec(memory_space=pltpu.VMEM) for _ in outs),
            scratch_shapes=list(scratch),
            compiler_params=pltpu.CompilerParams(vmem_limit_bytes=20 << 20),
            cost_estimate=pl.CostEstimate(flops=flops, bytes_accessed=nbytes, transcendentals=0),
        )(*args)

    return call


def tiled(kernel, grid, in_specs, outs, scratch, flops, nbytes, limit):
    def call(*args):
        return pl.pallas_call(
            kernel,
            grid=(grid,),
            out_shape=tuple(jax.ShapeDtypeStruct(s, d) for s, d, _, _ in outs),
            in_specs=[pl.BlockSpec(b, m) for b, m in in_specs],
            out_specs=tuple(pl.BlockSpec(b, m) for _, _, b, m in outs),
            scratch_shapes=list(scratch),
            compiler_params=pltpu.CompilerParams(
                vmem_limit_bytes=limit, dimension_semantics=("arbitrary",)
            ),
            cost_estimate=pl.CostEstimate(flops=flops, bytes_accessed=nbytes, transcendentals=0),
        )(*args)

    return call


def at2(i):
    return (0, i)


def at3(i):
    return (0, 0, i)


def fixed2(i):
    return (0, 0)


def dot(a, b, ca=1, cb=0):
    return lax.dot_general(a, b, (((ca,), (cb,)), ((), ())), preferred_element_type=F32)


def iota(shape, dim):
    return lax.broadcasted_iota(I32, shape, dim)


def send_kernel(pos_ref, frozen_ref, out_ref, sel_ref, in_buf, out_buf, in_sem, out_sem):
    rows = pos_ref.shape[1]
    slots = sel_ref.shape[0]
    parts, shards, cap, chans = out_buf.shape
    loads = [
        pltpu.make_async_copy(frozen_ref.at[a], in_buf.at[a], in_sem.at[a]) for a in range(parts)
    ]
    for load in loads:
        load.start()
    dest = (pos_ref[...] // rows).astype(F32)
    dest_row = jnp.broadcast_to(dest, (rows, rows))
    dest_col = dest_row.T
    earlier = (dest_row == dest_col) & (iota((rows, rows), 0) < iota((rows, rows), 1))
    rank = jnp.sum(jnp.where(earlier, 1.0, 0.0), axis=0, keepdims=True)
    slot = dest * float(cap) + rank
    sel = jnp.where(
        iota((slots, rows), 0).astype(F32) == jnp.broadcast_to(slot, (slots, rows)), 1.0, 0.0
    ).astype(BF)
    sel_ref[...] = sel
    stores = []
    for a in range(parts):
        loads[a].wait()
        for c in range(0, chans, 256):
            out_buf[a, :, :, c : c + 256] = (
                dot(sel, in_buf[a, :, c : c + 256]).astype(BF).reshape(shards, cap, 256)
            )
        store = pltpu.make_async_copy(
            out_buf.at[a], out_ref.at[:, :, pl.ds(a * chans, chans)], out_sem.at[a]
        )
        store.start()
        stores.append(store)
    for store in stores:
        store.wait()


def low_kernel(tok_ref, down_ref, out_ref):
    out_ref[...] = dot(down_ref[...], tok_ref[...], 1, 1)


def send_low_kernel(sel_ref, pos_ref, low_ref, out_ref):
    shards, cap, _ = out_ref.shape
    rank_dim, rows = low_ref.shape
    within = jnp.broadcast_to((pos_ref[...] % rows).astype(F32), (8, rows))
    mark = jnp.where(iota((8, rows), 0) == 0, within, 1.0)
    extra = jnp.concatenate([low_ref[...], mark, jnp.zeros((128 - 8 - rank_dim, rows), F32)])
    out_ref[...] = dot(sel_ref[...], extra.T.astype(BF)).astype(BF).reshape(shards, cap, 128)


def send_tokens_kernel(sel_ref, tok_ref, out_ref):
    shards, cap, chans = out_ref.shape
    for c in range(0, chans, 256):
        out_ref[:, :, c : c + 256] = (
            dot(sel_ref[...], tok_ref[:, c : c + 256]).astype(BF).reshape(shards, cap, 256)
        )


def shifted_down(value, edge0, edge1):
    row = iota(value.shape, 0)
    one = jnp.where(row == 0, edge1, pltpu.roll(value, 1, 0))
    two = jnp.where(row == 0, edge0, jnp.where(row == 1, edge1, pltpu.roll(value, 2, 0)))
    return one, two


def post_kernel(
    got0_ref, got1_ref, got2_ref, extra_ref, up_ref, taps_ref, offr_ref, cot_ref,
    pre_ref, post_ref, x_ref, b_ref, ahead_ref, behind_ref, place_ref, low_ref,
    ahead_edge, behind_edge, low_t_ref, mask_ref,
):
    parts, rows, width = pre_ref.shape
    slots = place_ref.shape[1]
    rank_dim = low_ref.shape[0]

    @pl.when(pl.program_id(0) == 0)
    def _():
        extra = extra_ref[...].reshape(slots, 128)
        mark = extra[:, rank_dim : rank_dim + 2].astype(F32)
        target = jnp.where(mark[:, 1:2] > 0.5, mark[:, 0:1], -1.0)
        place_t = jnp.where(
            jnp.broadcast_to(target, (slots, rows)) == iota((slots, rows), 1).astype(F32), 1.0, 0.0
        )
        place = place_t.T.astype(BF)
        place_ref[...] = place
        picked = dot(place, extra)
        low_t_ref[...] = picked[:, :rank_dim].astype(BF)
        low_ref[...] = picked.T[:rank_dim].astype(BF)
        for b in range(rows // 128):
            off = columns_of(offr_ref[:, 128 * b : 128 * b + 128])
            mask_ref[0, 128 * b : 128 * b + 128] = jnp.where(off >= 1.0, 1.0, 0.0)
            mask_ref[1, 128 * b : 128 * b + 128] = jnp.where(off >= 2.0, 1.0, 0.0)

    mask1 = jnp.concatenate([mask_ref[0]] * (width // 128), 1)
    mask2 = jnp.concatenate([mask_ref[1]] * (width // 128), 1)
    ahead_edge[...] = jnp.zeros_like(ahead_edge)
    behind_edge[...] = jnp.zeros_like(behind_edge)
    nothing = jnp.zeros((1, width), F32)
    made = []
    for a, got_ref in enumerate((got0_ref, got1_ref, got2_ref)):
        value = dot(place_ref[...], got_ref[...].reshape(slots, width)) + dot(low_t_ref[...], up_ref[a])
        value = value.astype(BF)
        pre_ref[a] = value
        value = value.astype(F32)
        ahead_edge[2 * a : 2 * a + 2] = value[rows - 2 :]
        behind_edge[2 * a : 2 * a + 2] = value[:2]
        one, two = shifted_down(value, nothing, nothing)
        total = (
            taps_ref[a : a + 1] * value
            + taps_ref[parts + a : parts + a + 1] * one * mask1
            + taps_ref[2 * parts + a : 2 * parts + a + 1] * two * mask2
        ).astype(BF)
        post_ref[a] = total
        made.append(total.astype(F32))
    product = (made[1] * made[2]).astype(BF)
    grad = cot_ref[...].astype(F32)
    back = (grad * made[0]).astype(BF)
    x_ref[...] = product
    b_ref[...] = back
    ahead_ref[:128] = product[rows - 128 :]
    behind_ref[:128] = back[:128]
    behind_edge[6:8] = grad[:2]
    behind_edge[8:9] = back[128:144].astype(F32)[:1]
    ahead_ref[128:] = ahead_edge[...].astype(BF)
    behind_ref[128:] = behind_edge[...].astype(BF)


def columns_of(row):
    return jnp.broadcast_to(row, (128, row.shape[1])).T


def bank_kernel(filt_ref, offr_ref, fwd_ref, adj_ref, mfwd_ref, madj_ref, frow_ref, grow_ref):
    blocks = offr_ref.shape[1] // 128 - 2
    sub, lane = iota((128, 128), 0), iota((128, 128), 1)

    @pl.when(pl.program_id(0) == 0)
    def _():
        for b in range(blocks + 1):
            first = 128 * b
            tall = 128 if b < blocks else 16
            prev, own = forward_masks(offr_ref, first)
            mfwd_ref[first : first + tall, :128] = prev.astype(BF)[:tall]
            mfwd_ref[first : first + tall, 128:] = own.astype(BF)[:tall]
            begin0 = (first + lane).astype(F32) - offr_ref[:, first : first + 128]
            begin1 = (first + 128 + lane).astype(F32) - offr_ref[:, first + 128 : first + 256]
            at = (first + sub).astype(F32)
            same = jnp.where((sub <= lane) & (at >= begin0), 1.0, 0.0).astype(BF)
            after = jnp.where((lane < sub) & (at >= begin1), 1.0, 0.0).astype(BF)
            madj_ref[first : first + tall, :128] = same[:tall]
            madj_ref[first : first + tall, 128:] = after[:tall]

    filt = filt_ref[...]
    flip = jnp.where((sub + lane) % 128 == 0, 1.0, 0.0).astype(BF)
    frow_ref[...] = filt.astype(F32)
    grow_ref[...] = dot(filt, flip)
    for g in range(8):
        f_row = jnp.broadcast_to(frow_ref[g : g + 1, :], (128, 128))
        g_row = jnp.broadcast_to(grow_ref[g : g + 1, :], (128, 128))
        circ = pltpu.roll(f_row, 0, 1, stride=1, stride_axis=0).astype(BF)
        circ_t = pltpu.roll(g_row, 0, 1, stride=1, stride_axis=0).astype(BF)
        two, two_t = jnp.concatenate([circ, circ], 1), jnp.concatenate([circ_t, circ_t], 1)
        for b in range(blocks + 1):
            tall = 128 if b < blocks else 16
            at = 1024 * b + tall * g
            fwd_ref[0, at : at + tall] = two_t[:tall] * mfwd_ref[128 * b : 128 * b + tall]
            adj_ref[0, at : at + tall] = two[:tall] * madj_ref[128 * b : 128 * b + tall]


def forward_masks(offr_ref, first):
    sub, lane = iota((128, 128), 0), iota((128, 128), 1)
    begin = (first + sub).astype(F32) - columns_of(offr_ref[:, first : first + 128])
    own = (lane <= sub) & ((first + lane).astype(F32) >= begin)
    prev = (lane > sub) & ((first - 128 + lane).astype(F32) >= begin)
    return jnp.where(prev, 1.0, 0.0), jnp.where(own, 1.0, 0.0)


def main_kernel(
    pre_ref, post_ref, x_ref, b_ref, prev_ref, next_ref, cot_ref, taps_ref, skip_ref, fwd_ref, adj_ref,
    offr_ref, low_ref, up_ref,
    mixer_ref, piece_ref, backlow_ref,
    mpair_ref, mask_ref, lhs_ref, rf_ref, ra_ref, rp_ref, bp_ref, total_ref,
):
    parts, rows, _ = pre_ref.shape
    step = pl.program_id(0)
    rank_dim = low_ref.shape[0]
    blocks = rows // 128
    sub, lane = iota((128, 128), 0), iota((128, 128), 1)
    turn = jnp.where(sub + lane == 127, 1.0, 0.0).astype(BF)

    @pl.when(step == 0)
    def _():
        total_ref[...] = jnp.zeros_like(total_ref)
        for b in range(blocks):
            prev, own = forward_masks(offr_ref, 128 * b)
            mpair_ref[b, :, :128] = dot(turn, prev.astype(BF))
            mpair_ref[b, :, 128:] = dot(turn, own.astype(BF))
        for b in range(blocks + 1):
            off = columns_of(offr_ref[:, 128 * b : 128 * b + 128])
            mask_ref[0, 128 * b : 128 * b + 128] = jnp.where(off >= 1.0, 1.0, 0.0)
            mask_ref[1, 128 * b : 128 * b + 128] = jnp.where(off >= 2.0, 1.0, 0.0)

    mask1, mask2 = mask_ref[0, :rows], mask_ref[1, :rows]
    next1, next2 = mask_ref[0, rows : rows + 16], mask_ref[1, rows : rows + 16]
    low = low_ref[...]
    row = iota((rows, 128), 0)
    top = iota((16, 128), 0) < 2
    lane_group = lane // 16
    piece_ref[...] = jnp.zeros_like(piece_ref)

    def tap(s, a):
        return taps_ref[s * parts + a : s * parts + a + 1]

    pedge = prev_ref[128:].astype(F32)
    nedge = next_ref[128:].astype(F32)
    heads, after = [], []
    for a in range(parts):
        head = pre_ref[a, :16].astype(F32)
        one, two = shifted_down(head, pedge[2 * a : 2 * a + 1], pedge[2 * a + 1 : 2 * a + 2])
        heads.append(
            (tap(0, a) * head + tap(1, a) * one * mask1[:16] + tap(2, a) * two * mask2[:16]).astype(BF)
        )
        tail = pre_ref[a, rows - 16 :].astype(F32)
        head = nedge if a == 0 else pltpu.roll(nedge, 16 - 2 * a, 0)
        one, two = shifted_down(head, tail[14:15], tail[15:16])
        after.append(
            (tap(0, a) * head + tap(1, a) * one * next1 + tap(2, a) * two * next2)
            .astype(BF)
            .astype(F32)
        )
    posts = [jnp.concatenate([heads[a], post_ref[a, 16:]]) for a in range(parts)]
    x_head = (heads[1].astype(F32) * heads[2].astype(F32)).astype(BF)
    b_head = (cot_ref[:16].astype(F32) * heads[0].astype(F32)).astype(BF)
    x_next = jnp.where(top, after[1] * after[2], 0.0).astype(BF)
    cot_next = pltpu.roll(nedge, 10, 0)
    b_next = jnp.where(top, cot_next * after[0], next_ref[:16].astype(F32)).astype(BF)
    b_last = jnp.where(iota((16, 128), 0) == 0, pltpu.roll(nedge, 8, 0), 0.0).astype(BF)
    blank = jnp.zeros((112, 128), BF)
    x_own = jnp.concatenate([x_head, x_ref[16:]])
    x_win = jnp.concatenate([prev_ref[:128], x_own, x_next, blank])
    b_win = jnp.concatenate(
        [b_head, b_ref[16:], b_next, next_ref[16:128], b_last, blank]
    )
    for b in range(blocks + 1):
        at = slice(1024 * b, 1024 * b + (1024 if b < blocks else 128))
        xw = x_win[128 * b : 128 * b + 256]
        rf_ref[at] = dot(fwd_ref[0, at], xw)
        ra_ref[at] = dot(adj_ref[0, at], b_win[128 * b : 128 * b + 256])
    backs = [dot(turn, b_win[128 * b : 128 * b + 128]) for b in range(blocks)]
    for g in range(8):
        part = jnp.zeros((128, 128), F32)
        for b in range(blocks):
            lhs = jnp.where(lane_group == g, backs[b], 0.0).astype(BF)
            pair = dot(lhs, x_win[128 * b : 128 * b + 256], 1, 1) * mpair_ref[b]
            part = part + pair[:, :128] + pair[:, 128:]
        part = pltpu.roll(part, 0, 1, stride=1, stride_axis=0)
        piece_ref[3, 0, 8 + g : 9 + g] = jnp.sum(part, axis=0, keepdims=True)
    skip = skip_ref[:]
    gsum = jnp.zeros((1, 128), F32)
    edges = None
    for b in range(blocks + 1):
        tall = 128 if b < blocks else 16
        conv = jnp.zeros((tall, 128), F32)
        adj = jnp.zeros((tall, 128), F32)
        for g in range(8):
            at = 1024 * b + tall * g
            conv = jnp.where(lane_group[:tall] == g, rf_ref[at : at + tall], conv)
            adj = jnp.where(lane_group[:tall] == g, ra_ref[at : at + tall], adj)
        at = slice(128 * b, 128 * b + 128)
        if b < blocks:
            query, key, value = (post[at].astype(F32) for post in posts)
            product = x_own[at].astype(F32)
            grad = cot_ref[at].astype(F32)
        else:
            query, key, value = after
            product = x_next.astype(F32)
            grad = cot_next
        direct = conv + skip * product
        gated = grad * query
        back = adj + skip * gated
        made = [(grad * direct).astype(BF), (back * value).astype(BF), (back * key).astype(BF)]
        if b < blocks:
            mixer_ref[at] = (query * direct).astype(BF)
            gsum = gsum + jnp.sum(gated * product, axis=0, keepdims=True)
            for a in range(parts):
                bp_ref[a, at] = made[a].astype(F32)
        else:
            edges = [m.astype(F32) for m in made]
    piece_ref[3, 0, 1:2] = gsum
    total = total_ref[...]
    for a in range(parts):
        post = bp_ref[a]
        edge0, edge1 = edges[a][0:1], edges[a][1:2]
        post1, post2 = post * mask1, post * mask2
        up1 = jnp.where(row == rows - 1, edge0 * next1[0:1], pltpu.roll(post1, rows - 1, 0))
        up2 = jnp.where(
            row == rows - 2,
            edge0 * next2[0:1],
            jnp.where(row == rows - 1, edge1 * next2[1:2], pltpu.roll(post2, rows - 2, 0)),
        )
        back_pre = (tap(0, a) * post + tap(1, a) * up1 + tap(2, a) * up2).astype(BF)
        pre = pre_ref[a, :].astype(F32)
        one, two = shifted_down(pre, pedge[2 * a : 2 * a + 1], pedge[2 * a + 1 : 2 * a + 2])
        sums = (
            jnp.sum(post * pre, axis=0, keepdims=True),
            jnp.sum(post1 * one, axis=0, keepdims=True),
            jnp.sum(post2 * two, axis=0, keepdims=True),
        )
        for t, value in enumerate(sums):
            k = t * parts + a
            if k < 8:
                piece_ref[2, 0, 16 + k : 17 + k] = value
            else:
                piece_ref[3, 0, 0:1] = value
        up_grad = dot(low, back_pre)
        if a == 0:
            piece_ref[0, 0, 16:24] = up_grad[:8]
            piece_ref[1, 0, :8] = up_grad[8:]
        elif a == 1:
            piece_ref[1, 0, 8:24] = up_grad
        else:
            piece_ref[2, 0, :16] = up_grad
        total = total + dot(up_ref[a, :], back_pre, 1, 1)
    total_ref[...] = total


    @pl.when(step == pl.num_programs(0) - 1)
    def _():
        for t in range(backlow_ref.shape[0]):
            backlow_ref[t] = total


def gather_kernel(lows_ref, got_ref, place_ref, sums_ref, out_ref):
    shards, cap, chans = got_ref.shape
    total = lows_ref[0]
    for t in range(1, lows_ref.shape[0]):
        total = total + lows_ref[t]
    placed = dot(total.astype(BF), place_ref[...]).astype(BF)
    down = jnp.concatenate(
        [
            dot(placed, got_ref[:, :, c : c + 256].reshape(shards * cap, 256))
            for c in range(0, chans, 256)
        ],
        1,
    )
    tiles = chans // 128
    for i in range(tiles):
        first = jnp.concatenate([down[:, 128 * i : 128 * i + 128], sums_ref[0, i, 16:]])
        out_ref[i] = first.astype(BF)
        for k in range(1, 4):
            out_ref[k * tiles + i] = sums_ref[k, i].astype(BF)


def sum_kernel(in_ref, out_ref):
    total = in_ref[0].astype(F32)
    for t in range(1, in_ref.shape[0]):
        total = total + in_ref[t].astype(F32)
    total = total.astype(BF)
    for t in range(out_ref.shape[0]):
        out_ref[t] = total


def spread_kernel(in_ref, down_ref, up_ref, short_ref, long_ref, gskip_ref):
    tiles = down_ref.shape[1] // 128
    flip = jnp.where(iota((128, 128), 0) + iota((128, 128), 1) == 127, 1.0, 0.0).astype(BF)
    for i in range(tiles):
        cols = slice(128 * i, 128 * i + 128)
        part = [in_ref[k * tiles + i].astype(F32) for k in range(4)]
        down_ref[:, cols] = part[0][:16]
        up_ref[0, :8, cols] = part[0][16:]
        up_ref[0, 8:, cols] = part[1][:8]
        up_ref[1, :, cols] = part[1][8:]
        up_ref[2, :, cols] = part[2][:16]
        for k in range(9):
            row = part[2][16 + k : 17 + k] if k < 8 else part[3][0:1]
            short_ref[k // 3, k % 3 : k % 3 + 1, cols] = row
        gskip_ref[i : i + 1] = part[3][1:2]
        long_ref[8 * i : 8 * i + 8] = dot(part[3][8:16].astype(BF), flip)


def swap(value, axis):
    return lax.all_to_all(value, axis, split_axis=0, concat_axis=0, tiled=True)


def neighbour(value, steps):
    count = lax.axis_size("ctx")
    pairs = [(i, i + steps) for i in range(count) if 0 <= i + steps < count]
    return lax.ppermute(value, "ctx", pairs)


def partner(value, axis, bit):
    return lax.ppermute(value, axis, [(i, i ^ bit) for i in range(lax.axis_size(axis))])


def doc_offsets(positions, lengths):
    index = jnp.arange(lengths.shape[0], dtype=I32)
    starts = jnp.sum(jnp.where(index[None, :] < index[:, None], lengths[None, :], 0), axis=1)
    begins = jnp.max(jnp.where(starts[None, :] <= positions[:, None], starts[None, :], 0), axis=1)
    return positions - begins


def on_device(
    tokens,
    frozen,
    cotangent,
    adapter_down_weight,
    adapter_up_weight,
    short_depthwise_filter,
    long_group_filter,
    skip_direct_scale,
    document_lengths,
    window_row_position,
):
    rows, chans = tokens.shape
    parts = frozen.shape[1]
    rank_dim = adapter_down_weight.shape[0]
    taps = short_depthwise_filter.shape[0]
    groups = long_group_filter.shape[0]
    shards = lax.axis_size("ctx")
    columns = lax.axis_size("tp")
    cap = 2 * rows // shards
    slots = shards * cap
    frozen = frozen.transpose(1, 0, 2)
    up = adapter_up_weight.transpose(1, 0, 2)
    pos_row = window_row_position.reshape(1, rows)
    vmem, far = pl.BlockSpec(memory_space=pltpu.VMEM), pl.BlockSpec(memory_space=pltpu.HBM)
    send, sel = pl.pallas_call(
        send_kernel,
        out_shape=(
            jax.ShapeDtypeStruct((shards, cap, parts * chans), BF),
            jax.ShapeDtypeStruct((slots, rows), BF),
        ),
        in_specs=[vmem, far],
        out_specs=(far, vmem),
        scratch_shapes=[
            pltpu.VMEM((parts, rows, chans), BF),
            pltpu.VMEM((parts, shards, cap, chans), BF),
            pltpu.SemaphoreType.DMA((parts,)),
            pltpu.SemaphoreType.DMA((parts,)),
        ],
        compiler_params=pltpu.CompilerParams(vmem_limit_bytes=66_000_000),
        cost_estimate=pl.CostEstimate(flops=1 << 30, bytes_accessed=5 << 20, transcendentals=0),
    )(pos_row, frozen)
    got = swap(send, "ctx")

    send, sel, document_lengths, short_depthwise_filter, adapter_down_weight = lax.optimization_barrier(
        (send, sel, document_lengths, short_depthwise_filter, adapter_down_weight)
    )
    (low_sum,) = whole(low_kernel, [((rank_dim, rows), F32)], flops=1 << 23, nbytes=1 << 19)(
        tokens, adapter_down_weight
    )
    for bit in range(3):
        low_sum = low_sum + partner(low_sum, "tp", 1 << bit)
    (send_low,) = whole(
        send_low_kernel, [((shards, cap, 128), BF)], flops=1 << 25, nbytes=1 << 19
    )(sel, pos_row, low_sum)
    (send_tok,) = whole(
        send_tokens_kernel, [((shards, cap, chans), BF)], flops=2 * slots * rows * chans, nbytes=2 << 20
    )(sel, tokens)
    first = lax.axis_index("ctx") * rows
    offsets = doc_offsets(first + jnp.arange(rows + 256, dtype=I32), document_lengths).astype(F32)
    off_row = offsets.reshape(1, rows + 256)
    tap_rows = short_depthwise_filter.reshape(taps * parts, chans).astype(F32)
    tap_rows = jnp.pad(tap_rows, ((0, 16 - taps * parts), (0, 0)))
    skip_row = skip_direct_scale.reshape(1, chans)
    blocks = rows // 128
    tall = 1024 * blocks + 128
    tiles = chans // 128
    fwd_bank, adj_bank = tiled(
        bank_kernel,
        tiles,
        [((8, 128), lambda i: (i, 0)), ((1, rows + 256), fixed2)],
        [((tiles, tall, 256), BF, (1, tall, 256), lambda i: (i, 0, 0))] * 2,
        [
            pltpu.VMEM((128 * blocks + 16, 256), BF),
            pltpu.VMEM((128 * blocks + 16, 256), BF),
            pltpu.VMEM((8, 128), F32),
            pltpu.VMEM((8, 128), F32),
        ],
        1 << 30,
        18 << 20,
        60_000_000,
    )(long_group_filter, off_row)
    got, send_low, send_tok, off_row, fwd_bank, adj_bank, tap_rows = lax.optimization_barrier(
        (got, send_low, send_tok, off_row, fwd_bank, adj_bank, tap_rows)
    )
    got_low = swap(send_low, "ctx")

    wide = 256
    steps = chans // wide
    pre, post, x, back, ahead, behind, place, low = tiled(
        post_kernel,
        steps,
        [((shards, cap, wide), lambda i, a=a: (0, 0, a * steps + i)) for a in range(parts)]
        + [
            ((shards, cap, 128), lambda i: (0, 0, 0)),
            ((parts, rank_dim, wide), at3),
            ((16, wide), at2),
            ((1, rows + 256), fixed2),
            ((rows, wide), at2),
        ],
        [
            ((parts, rows, chans), BF, (parts, rows, wide), at3),
            ((parts, rows, chans), BF, (parts, rows, wide), at3),
            ((rows, chans), BF, (rows, wide), at2),
            ((rows, chans), BF, (rows, wide), at2),
            ((144, chans), BF, (144, wide), at2),
            ((144, chans), BF, (144, wide), at2),
            ((rows, slots), BF, (rows, slots), fixed2),
            ((rank_dim, rows), BF, (rank_dim, rows), fixed2),
        ],
        [
            pltpu.VMEM((16, wide), F32),
            pltpu.VMEM((16, wide), F32),
            pltpu.VMEM((rows, rank_dim), BF),
            pltpu.VMEM((2, rows, 128), F32),
        ],
        1 << 30,
        8 << 20,
        60_000_000,
    )(got, got, got, got_low, up, tap_rows, off_row, cotangent)
    send_tok, ahead, behind = lax.optimization_barrier((send_tok, ahead, behind))
    from_prev = neighbour(ahead, 1)
    from_next = neighbour(behind, -1)
    got_tok = swap(send_tok, "ctx")
    mixer, sums, back_low_part = tiled(
        main_kernel,
        chans // 128,
        [
            ((parts, rows, 128), at3),
            ((parts, rows, 128), at3),
            ((rows, 128), at2),
            ((rows, 128), at2),
            ((144, 128), at2),
            ((144, 128), at2),
            ((rows, 128), at2),
            ((16, 128), at2),
            ((1, 128), at2),
            ((1, tall, 256), lambda i: (i, 0, 0)),
            ((1, tall, 256), lambda i: (i, 0, 0)),
            ((1, rows + 256), fixed2),
            ((rank_dim, rows), fixed2),
            ((parts, rank_dim, 128), at3),
        ],
        [
            ((rows, chans), BF, (rows, 128), at2),
            ((4, chans // 128, 24, 128), F32, (4, 1, 24, 128), lambda i: (0, i, 0, 0)),
            ((columns, rank_dim, rows), F32, (columns, rank_dim, rows), lambda i: (0, 0, 0)),
        ],
        [
            pltpu.VMEM((blocks, 128, 256), F32),
            pltpu.VMEM((2, rows + 128, 128), F32),
            pltpu.VMEM((1024, 128), BF),
            pltpu.VMEM((tall, 128), F32),
            pltpu.VMEM((tall, 128), F32),
            pltpu.VMEM((blocks, 1024, 256), F32),
            pltpu.VMEM((parts, rows, 128), F32),
            pltpu.VMEM((rank_dim, rows), F32),
        ],
        10 << 30,
        8 << 20,
        60_000_000,
    )(pre, post, x, back, from_prev, from_next, cotangent, tap_rows, skip_row, fwd_bank, adj_bank,
      off_row, low, up)
    got_tok, back_low_part = lax.optimization_barrier((got_tok, back_low_part))
    back_lows = swap(back_low_part, "tp")
    (pieces,) = whole(
        gather_kernel, [((shards, 24, 128), BF)], flops=1 << 26, nbytes=2 << 20
    )(back_lows, got_tok, place, sums)
    pieces = swap(pieces, "ctx")
    (pieces,) = whole(sum_kernel, [((shards, 24, 128), BF)], flops=1 << 20, nbytes=1 << 20)(pieces)
    pieces = swap(pieces, "ctx")
    grad_down, up_gradient, grad_short, grad_long, grad_skip = whole(
        spread_kernel,
        [
            ((rank_dim, chans), F32),
            ((parts, rank_dim, chans), F32),
            ((taps, parts, chans), F32),
            ((groups, 128), F32),
            ((chans // 128, 128), F32),
        ],
        flops=1 << 20,
        nbytes=1 << 20,
    )(pieces)
    return (
        mixer,
        grad_down,
        up_gradient.transpose(1, 0, 2),
        grad_short,
        grad_long,
        grad_skip.reshape(chans),
    )


def solution(mesh):
    placed = (
        P("ctx", "tp"),
        P("ctx", None, "tp"),
        P("ctx", "tp"),
        P(None, "tp"),
        P(None, None, "tp"),
        P(None, None, "tp"),
        P("tp", None),
        P("tp"),
        P(),
        P("ctx"),
    )
    return jax.shard_map(
        on_device,
        mesh=mesh,
        in_specs=placed,
        out_specs=(
            P("ctx", "tp"),
            P(None, "tp"),
            P(None, None, "tp"),
            P(None, None, "tp"),
            P("tp", None),
            P("tp"),
        ),
        check_vma=False,
    )
```

```python
import jax
import jax.numpy as jnp
from jax import lax
from jax.experimental import pallas as pl
from jax.experimental.pallas import tpu as pltpu
from jax.sharding import PartitionSpec as P

BF = jnp.bfloat16
F32 = jnp.float32
I32 = jnp.int32


def whole(kernel, outs, scratch=(), flops=0, nbytes=0):
    def call(*args):
        return pl.pallas_call(
            kernel,
            out_shape=tuple(jax.ShapeDtypeStruct(s, d) for s, d in outs),
            in_specs=[pl.BlockSpec(memory_space=pltpu.VMEM)] * len(args),
            out_specs=tuple(pl.BlockSpec(memory_space=pltpu.VMEM) for _ in outs),
            scratch_shapes=list(scratch),
            compiler_params=pltpu.CompilerParams(vmem_limit_bytes=20 << 20),
            cost_estimate=pl.CostEstimate(flops=flops, bytes_accessed=nbytes, transcendentals=0),
        )(*args)

    return call


def tiled(kernel, grid, in_specs, outs, scratch, flops, nbytes, limit):
    def call(*args):
        return pl.pallas_call(
            kernel,
            grid=(grid,),
            out_shape=tuple(jax.ShapeDtypeStruct(s, d) for s, d, _, _ in outs),
            in_specs=[pl.BlockSpec(b, m) for b, m in in_specs],
            out_specs=tuple(pl.BlockSpec(b, m) for _, _, b, m in outs),
            scratch_shapes=list(scratch),
            compiler_params=pltpu.CompilerParams(
                vmem_limit_bytes=limit, dimension_semantics=("arbitrary",)
            ),
            cost_estimate=pl.CostEstimate(flops=flops, bytes_accessed=nbytes, transcendentals=0),
        )(*args)

    return call


def at2(i):
    return (0, i)


def at3(i):
    return (0, 0, i)


def fixed2(i):
    return (0, 0)


def dot(a, b, ca=1, cb=0):
    return lax.dot_general(a, b, (((ca,), (cb,)), ((), ())), preferred_element_type=F32)


def iota(shape, dim):
    return lax.broadcasted_iota(I32, shape, dim)


def send_kernel(pos_ref, frozen_ref, out_ref, sel_ref, in_buf, out_buf, in_sem, out_sem):
    rows = pos_ref.shape[1]
    slots = sel_ref.shape[0]
    parts, shards, cap, chans = out_buf.shape
    half = chans // 2
    spans = [(a, c) for a in range(parts) for c in range(0, chans, half)]
    loads = [
        pltpu.make_async_copy(
            frozen_ref.at[a, :, pl.ds(c, half)], in_buf.at[a, :, pl.ds(c, half)], in_sem.at[k]
        )
        for k, (a, c) in enumerate(spans)
    ]
    for load in loads:
        load.start()
    dest = (pos_ref[...] // rows).astype(F32)
    dest_row = jnp.broadcast_to(dest, (rows, rows))
    dest_col = dest_row.T
    earlier = (dest_row == dest_col) & (iota((rows, rows), 0) < iota((rows, rows), 1))
    rank = jnp.sum(jnp.where(earlier, 1.0, 0.0), axis=0, keepdims=True)
    slot = dest * float(cap) + rank
    sel = jnp.where(
        iota((slots, rows), 0).astype(F32) == jnp.broadcast_to(slot, (slots, rows)), 1.0, 0.0
    ).astype(BF)
    sel_ref[...] = sel
    stores = []
    for k, (a, first) in enumerate(spans):
        loads[k].wait()
        for c in range(first, first + half, 256):
            out_buf[a, :, :, c : c + 256] = (
                dot(sel, in_buf[a, :, c : c + 256]).astype(BF).reshape(shards, cap, 256)
            )
        store = pltpu.make_async_copy(
            out_buf.at[a, :, :, pl.ds(first, half)],
            out_ref.at[:, :, pl.ds(a * chans + first, half)],
            out_sem.at[k],
        )
        store.start()
        stores.append(store)
    for store in stores:
        store.wait()


def low_kernel(tok_ref, down_ref, out_ref):
    out_ref[...] = dot(down_ref[...], tok_ref[...], 1, 1)


def send_low_kernel(sel_ref, pos_ref, low_ref, out_ref):
    shards, cap, _ = out_ref.shape
    rank_dim, rows = low_ref.shape
    within = jnp.broadcast_to((pos_ref[...] % rows).astype(F32), (8, rows))
    mark = jnp.where(iota((8, rows), 0) == 0, within, 1.0)
    extra = jnp.concatenate([low_ref[...], mark, jnp.zeros((128 - 8 - rank_dim, rows), F32)])
    out_ref[...] = dot(sel_ref[...], extra.T.astype(BF)).astype(BF).reshape(shards, cap, 128)


def send_tokens_kernel(sel_ref, tok_ref, out_ref):
    shards, cap, chans = out_ref.shape
    for c in range(0, chans, 256):
        out_ref[:, :, c : c + 256] = (
            dot(sel_ref[...], tok_ref[:, c : c + 256]).astype(BF).reshape(shards, cap, 256)
        )


def shifted_down(value, edge0, edge1):
    row = iota(value.shape, 0)
    one = jnp.where(row == 0, edge1, pltpu.roll(value, 1, 0))
    two = jnp.where(row == 0, edge0, jnp.where(row == 1, edge1, pltpu.roll(value, 2, 0)))
    return one, two


def post_kernel(
    got0_ref, got1_ref, got2_ref, extra_ref, up_ref, taps_ref, offr_ref, cot_ref,
    pre_ref, post_ref, x_ref, b_ref, ahead_ref, behind_ref, place_ref, low_ref,
    ahead_edge, behind_edge, low_t_ref, mask_ref,
):
    parts, rows, width = pre_ref.shape
    slots = place_ref.shape[1]
    rank_dim = low_ref.shape[0]

    @pl.when(pl.program_id(0) == 0)
    def _():
        extra = extra_ref[...].reshape(slots, 128)
        mark = extra[:, rank_dim : rank_dim + 2].astype(F32)
        target = jnp.where(mark[:, 1:2] > 0.5, mark[:, 0:1], -1.0)
        place_t = jnp.where(
            jnp.broadcast_to(target, (slots, rows)) == iota((slots, rows), 1).astype(F32), 1.0, 0.0
        )
        place = place_t.T.astype(BF)
        place_ref[...] = place
        picked = dot(place, extra)
        low_t_ref[...] = picked[:, :rank_dim].astype(BF)
        low_ref[...] = picked.T[:rank_dim].astype(BF)
        for b in range(rows // 128):
            off = columns_of(offr_ref[:, 128 * b : 128 * b + 128])
            mask_ref[0, 128 * b : 128 * b + 128] = jnp.where(off >= 1.0, 1.0, 0.0)
            mask_ref[1, 128 * b : 128 * b + 128] = jnp.where(off >= 2.0, 1.0, 0.0)

    mask1 = jnp.concatenate([mask_ref[0]] * (width // 128), 1)
    mask2 = jnp.concatenate([mask_ref[1]] * (width // 128), 1)
    ahead_edge[...] = jnp.zeros_like(ahead_edge)
    behind_edge[...] = jnp.zeros_like(behind_edge)
    nothing = jnp.zeros((1, width), F32)
    made = []
    for a, got_ref in enumerate((got0_ref, got1_ref, got2_ref)):
        value = dot(place_ref[...], got_ref[...].reshape(slots, width)) + dot(low_t_ref[...], up_ref[a])
        value = value.astype(BF)
        pre_ref[a] = value
        value = value.astype(F32)
        ahead_edge[2 * a : 2 * a + 2] = value[rows - 2 :]
        behind_edge[2 * a : 2 * a + 2] = value[:2]
        one, two = shifted_down(value, nothing, nothing)
        total = (
            taps_ref[a : a + 1] * value
            + taps_ref[parts + a : parts + a + 1] * one * mask1
            + taps_ref[2 * parts + a : 2 * parts + a + 1] * two * mask2
        ).astype(BF)
        post_ref[a] = total
        made.append(total.astype(F32))
    product = (made[1] * made[2]).astype(BF)
    grad = cot_ref[...].astype(F32)
    back = (grad * made[0]).astype(BF)
    x_ref[...] = product
    b_ref[...] = back
    ahead_ref[:128] = product[rows - 128 :]
    behind_ref[:128] = back[:128]
    behind_edge[6:8] = grad[:2]
    behind_edge[8:9] = back[128:144].astype(F32)[:1]
    ahead_ref[128:] = ahead_edge[...].astype(BF)
    behind_ref[128:] = behind_edge[...].astype(BF)


def columns_of(row):
    return jnp.broadcast_to(row, (128, row.shape[1])).T


def bank_kernel(filt_ref, offr_ref, fwd_ref, adj_ref, mfwd_ref, madj_ref, frow_ref, grow_ref):
    blocks = offr_ref.shape[1] // 128 - 2
    sub, lane = iota((128, 128), 0), iota((128, 128), 1)

    @pl.when(pl.program_id(0) == 0)
    def _():
        for b in range(blocks + 1):
            first = 128 * b
            tall = 128 if b < blocks else 16
            prev, own = forward_masks(offr_ref, first)
            mfwd_ref[first : first + tall, :128] = prev.astype(BF)[:tall]
            mfwd_ref[first : first + tall, 128:] = own.astype(BF)[:tall]
            begin0 = (first + lane).astype(F32) - offr_ref[:, first : first + 128]
            begin1 = (first + 128 + lane).astype(F32) - offr_ref[:, first + 128 : first + 256]
            at = (first + sub).astype(F32)
            same = jnp.where((sub <= lane) & (at >= begin0), 1.0, 0.0).astype(BF)
            after = jnp.where((lane < sub) & (at >= begin1), 1.0, 0.0).astype(BF)
            madj_ref[first : first + tall, :128] = same[:tall]
            madj_ref[first : first + tall, 128:] = after[:tall]

    filt = filt_ref[...]
    flip = jnp.where((sub + lane) % 128 == 0, 1.0, 0.0).astype(BF)
    frow_ref[...] = filt.astype(F32)
    grow_ref[...] = dot(filt, flip)
    for g in range(8):
        f_row = jnp.broadcast_to(frow_ref[g : g + 1, :], (128, 128))
        g_row = jnp.broadcast_to(grow_ref[g : g + 1, :], (128, 128))
        circ = pltpu.roll(f_row, 0, 1, stride=1, stride_axis=0).astype(BF)
        circ_t = pltpu.roll(g_row, 0, 1, stride=1, stride_axis=0).astype(BF)
        two, two_t = jnp.concatenate([circ, circ], 1), jnp.concatenate([circ_t, circ_t], 1)
        for b in range(blocks + 1):
            tall = 128 if b < blocks else 16
            at = 1024 * b + tall * g
            fwd_ref[0, at : at + tall] = two_t[:tall] * mfwd_ref[128 * b : 128 * b + tall]
            adj_ref[0, at : at + tall] = two[:tall] * madj_ref[128 * b : 128 * b + tall]


def forward_masks(offr_ref, first):
    sub, lane = iota((128, 128), 0), iota((128, 128), 1)
    begin = (first + sub).astype(F32) - columns_of(offr_ref[:, first : first + 128])
    own = (lane <= sub) & ((first + lane).astype(F32) >= begin)
    prev = (lane > sub) & ((first - 128 + lane).astype(F32) >= begin)
    return jnp.where(prev, 1.0, 0.0), jnp.where(own, 1.0, 0.0)


def main_kernel(
    pre_ref, post_ref, x_ref, b_ref, prev_ref, next_ref, cot_ref, taps_ref, skip_ref, fwd_ref, adj_ref,
    offr_ref, low_ref, up_ref,
    mixer_ref, piece_ref, backlow_ref,
    mpair_ref, mask_ref, lhs_ref, rf_ref, ra_ref, rp_ref, bp_ref, total_ref,
):
    parts, rows, _ = pre_ref.shape
    step = pl.program_id(0)
    rank_dim = low_ref.shape[0]
    blocks = rows // 128
    sub, lane = iota((128, 128), 0), iota((128, 128), 1)
    turn = jnp.where(sub + lane == 127, 1.0, 0.0).astype(BF)

    @pl.when(step == 0)
    def _():
        total_ref[...] = jnp.zeros_like(total_ref)
        for b in range(blocks):
            prev, own = forward_masks(offr_ref, 128 * b)
            mpair_ref[b, :, :128] = dot(turn, prev.astype(BF))
            mpair_ref[b, :, 128:] = dot(turn, own.astype(BF))
        for b in range(blocks + 1):
            off = columns_of(offr_ref[:, 128 * b : 128 * b + 128])
            mask_ref[0, 128 * b : 128 * b + 128] = jnp.where(off >= 1.0, 1.0, 0.0)
            mask_ref[1, 128 * b : 128 * b + 128] = jnp.where(off >= 2.0, 1.0, 0.0)

    mask1, mask2 = mask_ref[0, :rows], mask_ref[1, :rows]
    next1, next2 = mask_ref[0, rows : rows + 16], mask_ref[1, rows : rows + 16]
    low = low_ref[...]
    row = iota((rows, 128), 0)
    top = iota((16, 128), 0) < 2
    lane_group = lane // 16
    piece_ref[...] = jnp.zeros_like(piece_ref)

    def tap(s, a):
        return taps_ref[s * parts + a : s * parts + a + 1]

    pedge = prev_ref[128:].astype(F32)
    nedge = next_ref[128:].astype(F32)
    heads, after = [], []
    for a in range(parts):
        head = pre_ref[a, :16].astype(F32)
        one, two = shifted_down(head, pedge[2 * a : 2 * a + 1], pedge[2 * a + 1 : 2 * a + 2])
        heads.append(
            (tap(0, a) * head + tap(1, a) * one * mask1[:16] + tap(2, a) * two * mask2[:16]).astype(BF)
        )
        tail = pre_ref[a, rows - 16 :].astype(F32)
        head = nedge if a == 0 else pltpu.roll(nedge, 16 - 2 * a, 0)
        one, two = shifted_down(head, tail[14:15], tail[15:16])
        after.append(
            (tap(0, a) * head + tap(1, a) * one * next1 + tap(2, a) * two * next2)
            .astype(BF)
            .astype(F32)
        )
    posts = [jnp.concatenate([heads[a], post_ref[a, 16:]]) for a in range(parts)]
    x_head = (heads[1].astype(F32) * heads[2].astype(F32)).astype(BF)
    b_head = (cot_ref[:16].astype(F32) * heads[0].astype(F32)).astype(BF)
    x_next = jnp.where(top, after[1] * after[2], 0.0).astype(BF)
    cot_next = pltpu.roll(nedge, 10, 0)
    b_next = jnp.where(top, cot_next * after[0], next_ref[:16].astype(F32)).astype(BF)
    b_last = jnp.where(iota((16, 128), 0) == 0, pltpu.roll(nedge, 8, 0), 0.0).astype(BF)
    blank = jnp.zeros((112, 128), BF)
    x_own = jnp.concatenate([x_head, x_ref[16:]])
    x_win = jnp.concatenate([prev_ref[:128], x_own, x_next, blank])
    b_win = jnp.concatenate(
        [b_head, b_ref[16:], b_next, next_ref[16:128], b_last, blank]
    )
    for b in range(blocks + 1):
        at = slice(1024 * b, 1024 * b + (1024 if b < blocks else 128))
        xw = x_win[128 * b : 128 * b + 256]
        rf_ref[at] = dot(fwd_ref[0, at], xw)
        ra_ref[at] = dot(adj_ref[0, at], b_win[128 * b : 128 * b + 256])
    backs = [dot(turn, b_win[128 * b : 128 * b + 128]) for b in range(blocks)]
    for g in range(8):
        part = jnp.zeros((128, 128), F32)
        for b in range(blocks):
            lhs = jnp.where(lane_group == g, backs[b], 0.0).astype(BF)
            pair = dot(lhs, x_win[128 * b : 128 * b + 256], 1, 1) * mpair_ref[b]
            part = part + pair[:, :128] + pair[:, 128:]
        part = pltpu.roll(part, 0, 1, stride=1, stride_axis=0)
        piece_ref[3, 0, 8 + g : 9 + g] = jnp.sum(part, axis=0, keepdims=True)
    skip = skip_ref[:]
    gsum = jnp.zeros((1, 128), F32)
    edges = None
    for b in range(blocks + 1):
        tall = 128 if b < blocks else 16
        conv = jnp.zeros((tall, 128), F32)
        adj = jnp.zeros((tall, 128), F32)
        for g in range(8):
            at = 1024 * b + tall * g
            conv = jnp.where(lane_group[:tall] == g, rf_ref[at : at + tall], conv)
            adj = jnp.where(lane_group[:tall] == g, ra_ref[at : at + tall], adj)
        at = slice(128 * b, 128 * b + 128)
        if b < blocks:
            query, key, value = (post[at].astype(F32) for post in posts)
            product = x_own[at].astype(F32)
            grad = cot_ref[at].astype(F32)
        else:
            query, key, value = after
            product = x_next.astype(F32)
            grad = cot_next
        direct = conv + skip * product
        gated = grad * query
        back = adj + skip * gated
        made = [(grad * direct).astype(BF), (back * value).astype(BF), (back * key).astype(BF)]
        if b < blocks:
            mixer_ref[at] = (query * direct).astype(BF)
            gsum = gsum + jnp.sum(gated * product, axis=0, keepdims=True)
            for a in range(parts):
                bp_ref[a, at] = made[a].astype(F32)
        else:
            edges = [m.astype(F32) for m in made]
    piece_ref[3, 0, 1:2] = gsum
    total = total_ref[...]
    for a in range(parts):
        post = bp_ref[a]
        edge0, edge1 = edges[a][0:1], edges[a][1:2]
        post1, post2 = post * mask1, post * mask2
        up1 = jnp.where(row == rows - 1, edge0 * next1[0:1], pltpu.roll(post1, rows - 1, 0))
        up2 = jnp.where(
            row == rows - 2,
            edge0 * next2[0:1],
            jnp.where(row == rows - 1, edge1 * next2[1:2], pltpu.roll(post2, rows - 2, 0)),
        )
        back_pre = (tap(0, a) * post + tap(1, a) * up1 + tap(2, a) * up2).astype(BF)
        pre = pre_ref[a, :].astype(F32)
        one, two = shifted_down(pre, pedge[2 * a : 2 * a + 1], pedge[2 * a + 1 : 2 * a + 2])
        sums = (
            jnp.sum(post * pre, axis=0, keepdims=True),
            jnp.sum(post1 * one, axis=0, keepdims=True),
            jnp.sum(post2 * two, axis=0, keepdims=True),
        )
        for t, value in enumerate(sums):
            k = t * parts + a
            if k < 8:
                piece_ref[2, 0, 16 + k : 17 + k] = value
            else:
                piece_ref[3, 0, 0:1] = value
        up_grad = dot(low, back_pre)
        if a == 0:
            piece_ref[0, 0, 16:24] = up_grad[:8]
            piece_ref[1, 0, :8] = up_grad[8:]
        elif a == 1:
            piece_ref[1, 0, 8:24] = up_grad
        else:
            piece_ref[2, 0, :16] = up_grad
        total = total + dot(up_ref[a, :], back_pre, 1, 1)
    total_ref[...] = total


    @pl.when(step == pl.num_programs(0) - 1)
    def _():
        backlow_ref[...] = total


def gather_kernel(low_ref, rest_ref, got_ref, place_ref, sums_ref, out_ref):
    shards, cap, chans = got_ref.shape
    total = low_ref[...] + rest_ref[...]
    placed = dot(total.astype(BF), place_ref[...]).astype(BF)
    down = jnp.concatenate(
        [
            dot(placed, got_ref[:, :, c : c + 256].reshape(shards * cap, 256))
            for c in range(0, chans, 256)
        ],
        1,
    )
    tiles = chans // 128
    for i in range(tiles):
        first = jnp.concatenate([down[:, 128 * i : 128 * i + 128], sums_ref[0, i, 16:]])
        out_ref[i] = first.astype(BF)
        for k in range(1, 4):
            out_ref[k * tiles + i] = sums_ref[k, i].astype(BF)


def sum_kernel(in_ref, out_ref):
    total = in_ref[0].astype(F32)
    for t in range(1, in_ref.shape[0]):
        total = total + in_ref[t].astype(F32)
    total = total.astype(BF)
    for t in range(out_ref.shape[0]):
        out_ref[t] = total


def spread_kernel(in_ref, down_ref, up_ref, short_ref, long_ref, gskip_ref):
    tiles = down_ref.shape[1] // 128
    flip = jnp.where(iota((128, 128), 0) + iota((128, 128), 1) == 127, 1.0, 0.0).astype(BF)
    for i in range(tiles):
        cols = slice(128 * i, 128 * i + 128)
        part = [in_ref[k * tiles + i].astype(F32) for k in range(4)]
        down_ref[:, cols] = part[0][:16]
        up_ref[0, :8, cols] = part[0][16:]
        up_ref[0, 8:, cols] = part[1][:8]
        up_ref[1, :, cols] = part[1][8:]
        up_ref[2, :, cols] = part[2][:16]
        for k in range(9):
            row = part[2][16 + k : 17 + k] if k < 8 else part[3][0:1]
            short_ref[k // 3, k % 3 : k % 3 + 1, cols] = row
        gskip_ref[i : i + 1] = part[3][1:2]
        long_ref[8 * i : 8 * i + 8] = dot(part[3][8:16].astype(BF), flip)


def swap(value, axis):
    return lax.all_to_all(value, axis, split_axis=0, concat_axis=0, tiled=True)


def neighbour(value, steps):
    count = lax.axis_size("ctx")
    pairs = [(i, i + steps) for i in range(count) if 0 <= i + steps < count]
    return lax.ppermute(value, "ctx", pairs)


def partner(value, axis, bit):
    return lax.ppermute(value, axis, [(i, i ^ bit) for i in range(lax.axis_size(axis))])


def doc_offsets(positions, lengths):
    index = jnp.arange(lengths.shape[0], dtype=I32)
    starts = jnp.sum(jnp.where(index[None, :] < index[:, None], lengths[None, :], 0), axis=1)
    begins = jnp.max(jnp.where(starts[None, :] <= positions[:, None], starts[None, :], 0), axis=1)
    return positions - begins


def on_device(
    tokens,
    frozen,
    cotangent,
    adapter_down_weight,
    adapter_up_weight,
    short_depthwise_filter,
    long_group_filter,
    skip_direct_scale,
    document_lengths,
    window_row_position,
):
    rows, chans = tokens.shape
    parts = frozen.shape[1]
    rank_dim = adapter_down_weight.shape[0]
    taps = short_depthwise_filter.shape[0]
    groups = long_group_filter.shape[0]
    shards = lax.axis_size("ctx")
    cap = 2 * rows // shards
    slots = shards * cap
    frozen = frozen.transpose(1, 0, 2)
    up = adapter_up_weight.transpose(1, 0, 2)
    pos_row = window_row_position.reshape(1, rows)
    vmem, far = pl.BlockSpec(memory_space=pltpu.VMEM), pl.BlockSpec(memory_space=pltpu.HBM)
    send, sel = pl.pallas_call(
        send_kernel,
        out_shape=(
            jax.ShapeDtypeStruct((shards, cap, parts * chans), BF),
            jax.ShapeDtypeStruct((slots, rows), BF),
        ),
        in_specs=[vmem, far],
        out_specs=(far, vmem),
        scratch_shapes=[
            pltpu.VMEM((parts, rows, chans), BF),
            pltpu.VMEM((parts, shards, cap, chans), BF),
            pltpu.SemaphoreType.DMA((2 * parts,)),
            pltpu.SemaphoreType.DMA((2 * parts,)),
        ],
        compiler_params=pltpu.CompilerParams(vmem_limit_bytes=66_000_000),
        cost_estimate=pl.CostEstimate(flops=1 << 30, bytes_accessed=5 << 20, transcendentals=0),
    )(pos_row, frozen)
    got = swap(send, "ctx")

    send, sel, document_lengths, short_depthwise_filter, adapter_down_weight = lax.optimization_barrier(
        (send, sel, document_lengths, short_depthwise_filter, adapter_down_weight)
    )
    (low_sum,) = whole(low_kernel, [((rank_dim, rows), F32)], flops=1 << 23, nbytes=1 << 19)(
        tokens, adapter_down_weight
    )
    for bit in range(3):
        low_sum = low_sum + partner(low_sum, "tp", 1 << bit)
    (send_low,) = whole(
        send_low_kernel, [((shards, cap, 128), BF)], flops=1 << 25, nbytes=1 << 19
    )(sel, pos_row, low_sum)
    (send_tok,) = whole(
        send_tokens_kernel, [((shards, cap, chans), BF)], flops=2 * slots * rows * chans, nbytes=2 << 20
    )(sel, tokens)
    first = lax.axis_index("ctx") * rows
    offsets = doc_offsets(first + jnp.arange(rows + 256, dtype=I32), document_lengths).astype(F32)
    off_row = offsets.reshape(1, rows + 256)
    tap_rows = short_depthwise_filter.reshape(taps * parts, chans).astype(F32)
    tap_rows = jnp.pad(tap_rows, ((0, 16 - taps * parts), (0, 0)))
    skip_row = skip_direct_scale.reshape(1, chans)
    blocks = rows // 128
    tall = 1024 * blocks + 128
    tiles = chans // 128
    fwd_bank, adj_bank = tiled(
        bank_kernel,
        tiles,
        [((8, 128), lambda i: (i, 0)), ((1, rows + 256), fixed2)],
        [((tiles, tall, 256), BF, (1, tall, 256), lambda i: (i, 0, 0))] * 2,
        [
            pltpu.VMEM((128 * blocks + 16, 256), BF),
            pltpu.VMEM((128 * blocks + 16, 256), BF),
            pltpu.VMEM((8, 128), F32),
            pltpu.VMEM((8, 128), F32),
        ],
        1 << 30,
        18 << 20,
        60_000_000,
    )(long_group_filter, off_row)
    got, send_low, send_tok, off_row, fwd_bank, adj_bank, tap_rows = lax.optimization_barrier(
        (got, send_low, send_tok, off_row, fwd_bank, adj_bank, tap_rows)
    )
    got_low = swap(send_low, "ctx")

    wide = 512
    steps = chans // wide
    pre, post, x, back, ahead, behind, place, low = tiled(
        post_kernel,
        steps,
        [((shards, cap, wide), lambda i, a=a: (0, 0, a * steps + i)) for a in range(parts)]
        + [
            ((shards, cap, 128), lambda i: (0, 0, 0)),
            ((parts, rank_dim, wide), at3),
            ((16, wide), at2),
            ((1, rows + 256), fixed2),
            ((rows, wide), at2),
        ],
        [
            ((parts, rows, chans), BF, (parts, rows, wide), at3),
            ((parts, rows, chans), BF, (parts, rows, wide), at3),
            ((rows, chans), BF, (rows, wide), at2),
            ((rows, chans), BF, (rows, wide), at2),
            ((144, chans), BF, (144, wide), at2),
            ((144, chans), BF, (144, wide), at2),
            ((rows, slots), BF, (rows, slots), fixed2),
            ((rank_dim, rows), BF, (rank_dim, rows), fixed2),
        ],
        [
            pltpu.VMEM((16, wide), F32),
            pltpu.VMEM((16, wide), F32),
            pltpu.VMEM((rows, rank_dim), BF),
            pltpu.VMEM((2, rows, 128), F32),
        ],
        1 << 30,
        8 << 20,
        60_000_000,
    )(got, got, got, got_low, up, tap_rows, off_row, cotangent)
    send_tok, ahead, behind = lax.optimization_barrier((send_tok, ahead, behind))
    from_prev = neighbour(ahead, 1)
    from_next = neighbour(behind, -1)
    got_tok = swap(send_tok, "ctx")
    mixer, sums, back_low_part = tiled(
        main_kernel,
        chans // 128,
        [
            ((parts, rows, 128), at3),
            ((parts, rows, 128), at3),
            ((rows, 128), at2),
            ((rows, 128), at2),
            ((144, 128), at2),
            ((144, 128), at2),
            ((rows, 128), at2),
            ((16, 128), at2),
            ((1, 128), at2),
            ((1, tall, 256), lambda i: (i, 0, 0)),
            ((1, tall, 256), lambda i: (i, 0, 0)),
            ((1, rows + 256), fixed2),
            ((rank_dim, rows), fixed2),
            ((parts, rank_dim, 128), at3),
        ],
        [
            ((rows, chans), BF, (rows, 128), at2),
            ((4, chans // 128, 24, 128), F32, (4, 1, 24, 128), lambda i: (0, i, 0, 0)),
            ((rank_dim, rows), F32, (rank_dim, rows), fixed2),
        ],
        [
            pltpu.VMEM((blocks, 128, 256), F32),
            pltpu.VMEM((2, rows + 128, 128), F32),
            pltpu.VMEM((1024, 128), BF),
            pltpu.VMEM((tall, 128), F32),
            pltpu.VMEM((tall, 128), F32),
            pltpu.VMEM((blocks, 1024, 256), F32),
            pltpu.VMEM((parts, rows, 128), F32),
            pltpu.VMEM((rank_dim, rows), F32),
        ],
        10 << 30,
        8 << 20,
        60_000_000,
    )(pre, post, x, back, from_prev, from_next, cotangent, tap_rows, skip_row, fwd_bank, adj_bank,
      off_row, low, up)
    got_tok, back_low_part = lax.optimization_barrier((got_tok, back_low_part))
    back_low = back_low_part
    for bit in range(2):
        back_low = back_low + partner(back_low, "tp", 1 << bit)
    back_low_rest = partner(back_low, "tp", 4)
    (pieces,) = whole(
        gather_kernel, [((shards, 24, 128), BF)], flops=1 << 26, nbytes=2 << 20
    )(back_low, back_low_rest, got_tok, place, sums)
    pieces = swap(pieces, "ctx")
    (pieces,) = whole(sum_kernel, [((shards, 24, 128), BF)], flops=1 << 20, nbytes=1 << 20)(pieces)
    pieces = swap(pieces, "ctx")
    grad_down, up_gradient, grad_short, grad_long, grad_skip = whole(
        spread_kernel,
        [
            ((rank_dim, chans), F32),
            ((parts, rank_dim, chans), F32),
            ((taps, parts, chans), F32),
            ((groups, 128), F32),
            ((chans // 128, 128), F32),
        ],
        flops=1 << 20,
        nbytes=1 << 20,
    )(pieces)
    return (
        mixer,
        grad_down,
        up_gradient.transpose(1, 0, 2),
        grad_short,
        grad_long,
        grad_skip.reshape(chans),
    )


def solution(mesh):
    placed = (
        P("ctx", "tp"),
        P("ctx", None, "tp"),
        P("ctx", "tp"),
        P(None, "tp"),
        P(None, None, "tp"),
        P(None, None, "tp"),
        P("tp", None),
        P("tp"),
        P(),
        P("ctx"),
    )
    return jax.shard_map(
        on_device,
        mesh=mesh,
        in_specs=placed,
        out_specs=(
            P("ctx", "tp"),
            P(None, "tp"),
            P(None, None, "tp"),
            P(None, None, "tp"),
            P("tp", None),
            P("tp"),
        ),
        check_vma=False,
    )
```

```python
import jax
import jax.numpy as jnp
from jax import lax
from jax.experimental import pallas as pl
from jax.experimental.pallas import tpu as pltpu
from jax.sharding import PartitionSpec as P

BF = jnp.bfloat16
F32 = jnp.float32
I32 = jnp.int32


def whole(kernel, outs, scratch=(), flops=0, nbytes=0):
    def call(*args):
        return pl.pallas_call(
            kernel,
            out_shape=tuple(jax.ShapeDtypeStruct(s, d) for s, d in outs),
            in_specs=[pl.BlockSpec(memory_space=pltpu.VMEM)] * len(args),
            out_specs=tuple(pl.BlockSpec(memory_space=pltpu.VMEM) for _ in outs),
            scratch_shapes=list(scratch),
            compiler_params=pltpu.CompilerParams(vmem_limit_bytes=20 << 20),
            cost_estimate=pl.CostEstimate(flops=flops, bytes_accessed=nbytes, transcendentals=0),
        )(*args)

    return call


def tiled(kernel, grid, in_specs, outs, scratch, flops, nbytes, limit):
    def call(*args):
        return pl.pallas_call(
            kernel,
            grid=(grid,),
            out_shape=tuple(jax.ShapeDtypeStruct(s, d) for s, d, _, _ in outs),
            in_specs=[pl.BlockSpec(b, m) for b, m in in_specs],
            out_specs=tuple(pl.BlockSpec(b, m) for _, _, b, m in outs),
            scratch_shapes=list(scratch),
            compiler_params=pltpu.CompilerParams(
                vmem_limit_bytes=limit, dimension_semantics=("arbitrary",)
            ),
            cost_estimate=pl.CostEstimate(flops=flops, bytes_accessed=nbytes, transcendentals=0),
        )(*args)

    return call


def at2(i):
    return (0, i)


def at3(i):
    return (0, 0, i)


def fixed2(i):
    return (0, 0)


def dot(a, b, ca=1, cb=0):
    return lax.dot_general(a, b, (((ca,), (cb,)), ((), ())), preferred_element_type=F32)


def iota(shape, dim):
    return lax.broadcasted_iota(I32, shape, dim)


def send_kernel(pos_ref, frozen_ref, out_ref, sel_ref, in_buf, out_buf, in_sem, out_sem):
    rows = pos_ref.shape[1]
    slots = sel_ref.shape[0]
    parts, shards, cap, chans = out_buf.shape
    loads = [
        pltpu.make_async_copy(frozen_ref.at[a], in_buf.at[a], in_sem.at[a]) for a in range(parts)
    ]
    for load in loads:
        load.start()
    dest = (pos_ref[...] // rows).astype(F32)
    dest_row = jnp.broadcast_to(dest, (rows, rows))
    dest_col = dest_row.T
    earlier = (dest_row == dest_col) & (iota((rows, rows), 0) < iota((rows, rows), 1))
    rank = jnp.sum(jnp.where(earlier, 1.0, 0.0), axis=0, keepdims=True)
    slot = dest * float(cap) + rank
    sel = jnp.where(
        iota((slots, rows), 0).astype(F32) == jnp.broadcast_to(slot, (slots, rows)), 1.0, 0.0
    ).astype(BF)
    sel_ref[...] = sel
    stores = []
    for a in range(parts):
        loads[a].wait()
        for c in range(0, chans, 256):
            out_buf[a, :, :, c : c + 256] = (
                dot(sel, in_buf[a, :, c : c + 256]).astype(BF).reshape(shards, cap, 256)
            )
        store = pltpu.make_async_copy(
            out_buf.at[a], out_ref.at[:, :, pl.ds(a * chans, chans)], out_sem.at[a]
        )
        store.start()
        stores.append(store)
    for store in stores:
        store.wait()


def low_kernel(tok_ref, down_ref, out_ref):
    out_ref[...] = dot(down_ref[...], tok_ref[...], 1, 1)


def send_low_kernel(sel_ref, pos_ref, low_ref, out_ref):
    shards, cap, _ = out_ref.shape
    rank_dim, rows = low_ref.shape
    within = jnp.broadcast_to((pos_ref[...] % rows).astype(F32), (8, rows))
    mark = jnp.where(iota((8, rows), 0) == 0, within, 1.0)
    extra = jnp.concatenate([low_ref[...], mark, jnp.zeros((128 - 8 - rank_dim, rows), F32)])
    out_ref[...] = dot(sel_ref[...], extra.T.astype(BF)).astype(BF).reshape(shards, cap, 128)


def send_tokens_kernel(sel_ref, tok_ref, out_ref):
    shards, cap, chans = out_ref.shape
    for c in range(0, chans, 256):
        out_ref[:, :, c : c + 256] = (
            dot(sel_ref[...], tok_ref[:, c : c + 256]).astype(BF).reshape(shards, cap, 256)
        )


def shifted_down(value, edge0, edge1):
    row = iota(value.shape, 0)
    one = jnp.where(row == 0, edge1, pltpu.roll(value, 1, 0))
    two = jnp.where(row == 0, edge0, jnp.where(row == 1, edge1, pltpu.roll(value, 2, 0)))
    return one, two


def post_kernel(
    got0_ref, got1_ref, got2_ref, extra_ref, up_ref, taps_ref, offr_ref, cot_ref,
    pre_ref, post_ref, x_ref, b_ref, ahead_ref, behind_ref, place_ref, low_ref,
    ahead_edge, behind_edge, low_t_ref, mask_ref,
):
    parts, rows, width = pre_ref.shape
    slots = place_ref.shape[1]
    rank_dim = low_ref.shape[0]

    @pl.when(pl.program_id(0) == 0)
    def _():
        extra = extra_ref[...].reshape(slots, 128)
        mark = extra[:, rank_dim : rank_dim + 2].astype(F32)
        target = jnp.where(mark[:, 1:2] > 0.5, mark[:, 0:1], -1.0)
        place_t = jnp.where(
            jnp.broadcast_to(target, (slots, rows)) == iota((slots, rows), 1).astype(F32), 1.0, 0.0
        )
        place = place_t.T.astype(BF)
        place_ref[...] = place
        picked = dot(place, extra)
        low_t_ref[...] = picked[:, :rank_dim].astype(BF)
        low_ref[...] = picked.T[:rank_dim].astype(BF)
        for b in range(rows // 128):
            off = columns_of(offr_ref[:, 128 * b : 128 * b + 128])
            mask_ref[0, 128 * b : 128 * b + 128] = jnp.where(off >= 1.0, 1.0, 0.0)
            mask_ref[1, 128 * b : 128 * b + 128] = jnp.where(off >= 2.0, 1.0, 0.0)

    mask1 = jnp.concatenate([mask_ref[0]] * (width // 128), 1)
    mask2 = jnp.concatenate([mask_ref[1]] * (width // 128), 1)
    ahead_edge[...] = jnp.zeros_like(ahead_edge)
    behind_edge[...] = jnp.zeros_like(behind_edge)
    nothing = jnp.zeros((1, width), F32)
    made = []
    for a, got_ref in enumerate((got0_ref, got1_ref, got2_ref)):
        value = dot(place_ref[...], got_ref[...].reshape(slots, width)) + dot(low_t_ref[...], up_ref[a])
        value = value.astype(BF)
        pre_ref[a] = value
        value = value.astype(F32)
        ahead_edge[2 * a : 2 * a + 2] = value[rows - 2 :]
        behind_edge[2 * a : 2 * a + 2] = value[:2]
        one, two = shifted_down(value, nothing, nothing)
        total = (
            taps_ref[a : a + 1] * value
            + taps_ref[parts + a : parts + a + 1] * one * mask1
            + taps_ref[2 * parts + a : 2 * parts + a + 1] * two * mask2
        ).astype(BF)
        post_ref[a] = total
        made.append(total.astype(F32))
    product = (made[1] * made[2]).astype(BF)
    grad = cot_ref[...].astype(F32)
    back = (grad * made[0]).astype(BF)
    x_ref[...] = product
    b_ref[...] = back
    ahead_ref[:128] = product[rows - 128 :]
    behind_ref[:128] = back[:128]
    behind_edge[6:8] = grad[:2]
    behind_edge[8:9] = back[128:144].astype(F32)[:1]
    ahead_ref[128:] = ahead_edge[...].astype(BF)
    behind_ref[128:] = behind_edge[...].astype(BF)


def columns_of(row):
    return jnp.broadcast_to(row, (128, row.shape[1])).T


def bank_kernel(filt_ref, offr_ref, fwd_ref, adj_ref, mfwd_ref, madj_ref, frow_ref, grow_ref):
    blocks = offr_ref.shape[1] // 128 - 2
    sub, lane = iota((128, 128), 0), iota((128, 128), 1)

    @pl.when(pl.program_id(0) == 0)
    def _():
        for b in range(blocks + 1):
            first = 128 * b
            tall = 128 if b < blocks else 16
            prev, own = forward_masks(offr_ref, first)
            mfwd_ref[first : first + tall, :128] = prev.astype(BF)[:tall]
            mfwd_ref[first : first + tall, 128:] = own.astype(BF)[:tall]
            begin0 = (first + lane).astype(F32) - offr_ref[:, first : first + 128]
            begin1 = (first + 128 + lane).astype(F32) - offr_ref[:, first + 128 : first + 256]
            at = (first + sub).astype(F32)
            same = jnp.where((sub <= lane) & (at >= begin0), 1.0, 0.0).astype(BF)
            after = jnp.where((lane < sub) & (at >= begin1), 1.0, 0.0).astype(BF)
            madj_ref[first : first + tall, :128] = same[:tall]
            madj_ref[first : first + tall, 128:] = after[:tall]

    filt = filt_ref[...]
    flip = jnp.where((sub + lane) % 128 == 0, 1.0, 0.0).astype(BF)
    frow_ref[...] = filt.astype(F32)
    grow_ref[...] = dot(filt, flip)
    for g in range(8):
        f_row = jnp.broadcast_to(frow_ref[g : g + 1, :], (128, 128))
        g_row = jnp.broadcast_to(grow_ref[g : g + 1, :], (128, 128))
        circ = pltpu.roll(f_row, 0, 1, stride=1, stride_axis=0).astype(BF)
        circ_t = pltpu.roll(g_row, 0, 1, stride=1, stride_axis=0).astype(BF)
        two, two_t = jnp.concatenate([circ, circ], 1), jnp.concatenate([circ_t, circ_t], 1)
        for b in range(blocks + 1):
            tall = 128 if b < blocks else 16
            at = 1024 * b + tall * g
            fwd_ref[0, at : at + tall] = two_t[:tall] * mfwd_ref[128 * b : 128 * b + tall]
            adj_ref[0, at : at + tall] = two[:tall] * madj_ref[128 * b : 128 * b + tall]


def forward_masks(offr_ref, first):
    sub, lane = iota((128, 128), 0), iota((128, 128), 1)
    begin = (first + sub).astype(F32) - columns_of(offr_ref[:, first : first + 128])
    own = (lane <= sub) & ((first + lane).astype(F32) >= begin)
    prev = (lane > sub) & ((first - 128 + lane).astype(F32) >= begin)
    return jnp.where(prev, 1.0, 0.0), jnp.where(own, 1.0, 0.0)


def main_kernel(
    pre_ref, post_ref, x_ref, b_ref, prev_ref, next_ref, cot_ref, taps_ref, skip_ref, fwd_ref, adj_ref,
    offr_ref, low_ref, up_ref,
    mixer_ref, piece_ref, backlow_ref,
    mpair_ref, mask_ref, lhs_ref, rf_ref, ra_ref, rp_ref, bp_ref, total_ref,
):
    parts, rows, _ = pre_ref.shape
    step = pl.program_id(0)
    rank_dim = low_ref.shape[0]
    blocks = rows // 128
    sub, lane = iota((128, 128), 0), iota((128, 128), 1)
    turn = jnp.where(sub + lane == 127, 1.0, 0.0).astype(BF)

    @pl.when(step == 0)
    def _():
        total_ref[...] = jnp.zeros_like(total_ref)
        for b in range(blocks):
            prev, own = forward_masks(offr_ref, 128 * b)
            mpair_ref[b, :, :128] = dot(turn, prev.astype(BF))
            mpair_ref[b, :, 128:] = dot(turn, own.astype(BF))
        for b in range(blocks + 1):
            off = columns_of(offr_ref[:, 128 * b : 128 * b + 128])
            mask_ref[0, 128 * b : 128 * b + 128] = jnp.where(off >= 1.0, 1.0, 0.0)
            mask_ref[1, 128 * b : 128 * b + 128] = jnp.where(off >= 2.0, 1.0, 0.0)

    mask1, mask2 = mask_ref[0, :rows], mask_ref[1, :rows]
    next1, next2 = mask_ref[0, rows : rows + 16], mask_ref[1, rows : rows + 16]
    low = low_ref[...]
    row = iota((rows, 128), 0)
    top = iota((16, 128), 0) < 2
    lane_group = lane // 16
    piece_ref[...] = jnp.zeros_like(piece_ref)

    def tap(s, a):
        return taps_ref[s * parts + a : s * parts + a + 1]

    pedge = prev_ref[128:].astype(F32)
    nedge = next_ref[128:].astype(F32)
    heads, after = [], []
    for a in range(parts):
        head = pre_ref[a, :16].astype(F32)
        one, two = shifted_down(head, pedge[2 * a : 2 * a + 1], pedge[2 * a + 1 : 2 * a + 2])
        heads.append(
            (tap(0, a) * head + tap(1, a) * one * mask1[:16] + tap(2, a) * two * mask2[:16]).astype(BF)
        )
        tail = pre_ref[a, rows - 16 :].astype(F32)
        head = nedge if a == 0 else pltpu.roll(nedge, 16 - 2 * a, 0)
        one, two = shifted_down(head, tail[14:15], tail[15:16])
        after.append(
            (tap(0, a) * head + tap(1, a) * one * next1 + tap(2, a) * two * next2)
            .astype(BF)
            .astype(F32)
        )
    posts = [jnp.concatenate([heads[a], post_ref[a, 16:]]) for a in range(parts)]
    x_head = (heads[1].astype(F32) * heads[2].astype(F32)).astype(BF)
    b_head = (cot_ref[:16].astype(F32) * heads[0].astype(F32)).astype(BF)
    x_next = jnp.where(top, after[1] * after[2], 0.0).astype(BF)
    cot_next = pltpu.roll(nedge, 10, 0)
    b_next = jnp.where(top, cot_next * after[0], next_ref[:16].astype(F32)).astype(BF)
    b_last = jnp.where(iota((16, 128), 0) == 0, pltpu.roll(nedge, 8, 0), 0.0).astype(BF)
    blank = jnp.zeros((112, 128), BF)
    x_own = jnp.concatenate([x_head, x_ref[16:]])
    x_win = jnp.concatenate([prev_ref[:128], x_own, x_next, blank])
    b_win = jnp.concatenate(
        [b_head, b_ref[16:], b_next, next_ref[16:128], b_last, blank]
    )
    for b in range(blocks + 1):
        at = slice(1024 * b, 1024 * b + (1024 if b < blocks else 128))
        xw = x_win[128 * b : 128 * b + 256]
        rf_ref[at] = dot(fwd_ref[0, at], xw)
        ra_ref[at] = dot(adj_ref[0, at], b_win[128 * b : 128 * b + 256])
    backs = [dot(turn, b_win[128 * b : 128 * b + 128]) for b in range(blocks)]
    for g in range(8):
        part = jnp.zeros((128, 128), F32)
        for b in range(blocks):
            lhs = jnp.where(lane_group == g, backs[b], 0.0).astype(BF)
            pair = dot(lhs, x_win[128 * b : 128 * b + 256], 1, 1) * mpair_ref[b]
            part = part + pair[:, :128] + pair[:, 128:]
        part = pltpu.roll(part, 0, 1, stride=1, stride_axis=0)
        piece_ref[3, 0, 8 + g : 9 + g] = jnp.sum(part, axis=0, keepdims=True)
    skip = skip_ref[:]
    gsum = jnp.zeros((1, 128), F32)
    edges = None
    for b in range(blocks + 1):
        tall = 128 if b < blocks else 16
        conv = jnp.zeros((tall, 128), F32)
        adj = jnp.zeros((tall, 128), F32)
        for g in range(8):
            at = 1024 * b + tall * g
            conv = jnp.where(lane_group[:tall] == g, rf_ref[at : at + tall], conv)
            adj = jnp.where(lane_group[:tall] == g, ra_ref[at : at + tall], adj)
        at = slice(128 * b, 128 * b + 128)
        if b < blocks:
            query, key, value = (post[at].astype(F32) for post in posts)
            product = x_own[at].astype(F32)
            grad = cot_ref[at].astype(F32)
        else:
            query, key, value = after
            product = x_next.astype(F32)
            grad = cot_next
        direct = conv + skip * product
        gated = grad * query
        back = adj + skip * gated
        made = [(grad * direct).astype(BF), (back * value).astype(BF), (back * key).astype(BF)]
        if b < blocks:
            mixer_ref[at] = (query * direct).astype(BF)
            gsum = gsum + jnp.sum(gated * product, axis=0, keepdims=True)
            for a in range(parts):
                bp_ref[a, at] = made[a].astype(F32)
        else:
            edges = [m.astype(F32) for m in made]
    piece_ref[3, 0, 1:2] = gsum
    total = total_ref[...]
    for a in range(parts):
        post = bp_ref[a]
        edge0, edge1 = edges[a][0:1], edges[a][1:2]
        post1, post2 = post * mask1, post * mask2
        up1 = jnp.where(row == rows - 1, edge0 * next1[0:1], pltpu.roll(post1, rows - 1, 0))
        up2 = jnp.where(
            row == rows - 2,
            edge0 * next2[0:1],
            jnp.where(row == rows - 1, edge1 * next2[1:2], pltpu.roll(post2, rows - 2, 0)),
        )
        back_pre = (tap(0, a) * post + tap(1, a) * up1 + tap(2, a) * up2).astype(BF)
        pre = pre_ref[a, :].astype(F32)
        one, two = shifted_down(pre, pedge[2 * a : 2 * a + 1], pedge[2 * a + 1 : 2 * a + 2])
        sums = (
            jnp.sum(post * pre, axis=0, keepdims=True),
            jnp.sum(post1 * one, axis=0, keepdims=True),
            jnp.sum(post2 * two, axis=0, keepdims=True),
        )
        for t, value in enumerate(sums):
            k = t * parts + a
            if k < 8:
                piece_ref[2, 0, 16 + k : 17 + k] = value
            else:
                piece_ref[3, 0, 0:1] = value
        up_grad = dot(low, back_pre)
        if a == 0:
            piece_ref[0, 0, 16:24] = up_grad[:8]
            piece_ref[1, 0, :8] = up_grad[8:]
        elif a == 1:
            piece_ref[1, 0, 8:24] = up_grad
        else:
            piece_ref[2, 0, :16] = up_grad
        total = total + dot(up_ref[a, :], back_pre, 1, 1)
    total_ref[...] = total


    @pl.when(step == pl.num_programs(0) - 1)
    def _():
        for t in range(backlow_ref.shape[0]):
            backlow_ref[t] = total


def gather_kernel(lows_ref, got_ref, place_ref, sums_ref, out_ref):
    shards, cap, chans = got_ref.shape
    total = lows_ref[0]
    for t in range(1, lows_ref.shape[0]):
        total = total + lows_ref[t]
    placed = dot(total.astype(BF), place_ref[...]).astype(BF)
    down = jnp.concatenate(
        [
            dot(placed, got_ref[:, :, c : c + 256].reshape(shards * cap, 256))
            for c in range(0, chans, 256)
        ],
        1,
    )
    tiles = chans // 128
    for i in range(tiles):
        first = jnp.concatenate([down[:, 128 * i : 128 * i + 128], sums_ref[0, i, 16:]])
        out_ref[i] = first.astype(BF)
        for k in range(1, 4):
            out_ref[k * tiles + i] = sums_ref[k, i].astype(BF)


def sum_kernel(in_ref, out_ref):
    total = in_ref[0].astype(F32)
    for t in range(1, in_ref.shape[0]):
        total = total + in_ref[t].astype(F32)
    total = total.astype(BF)
    for t in range(out_ref.shape[0]):
        out_ref[t] = total


def spread_kernel(in_ref, down_ref, up_ref, short_ref, long_ref, gskip_ref):
    tiles = down_ref.shape[1] // 128
    flip = jnp.where(iota((128, 128), 0) + iota((128, 128), 1) == 127, 1.0, 0.0).astype(BF)
    for i in range(tiles):
        cols = slice(128 * i, 128 * i + 128)
        part = [in_ref[k * tiles + i].astype(F32) for k in range(4)]
        down_ref[:, cols] = part[0][:16]
        up_ref[0, :8, cols] = part[0][16:]
        up_ref[0, 8:, cols] = part[1][:8]
        up_ref[1, :, cols] = part[1][8:]
        up_ref[2, :, cols] = part[2][:16]
        for k in range(9):
            row = part[2][16 + k : 17 + k] if k < 8 else part[3][0:1]
            short_ref[k // 3, k % 3 : k % 3 + 1, cols] = row
        gskip_ref[i : i + 1] = part[3][1:2]
        long_ref[8 * i : 8 * i + 8] = dot(part[3][8:16].astype(BF), flip)


def swap(value, axis):
    return lax.all_to_all(value, axis, split_axis=0, concat_axis=0, tiled=True)


def neighbour(value, steps):
    count = lax.axis_size("ctx")
    pairs = [(i, i + steps) for i in range(count) if 0 <= i + steps < count]
    return lax.ppermute(value, "ctx", pairs)


def partner(value, axis, bit):
    return lax.ppermute(value, axis, [(i, i ^ bit) for i in range(lax.axis_size(axis))])


def doc_offsets(positions, lengths):
    index = jnp.arange(lengths.shape[0], dtype=I32)
    starts = jnp.sum(jnp.where(index[None, :] < index[:, None], lengths[None, :], 0), axis=1)
    begins = jnp.max(jnp.where(starts[None, :] <= positions[:, None], starts[None, :], 0), axis=1)
    return positions - begins


def on_device(
    tokens,
    frozen,
    cotangent,
    adapter_down_weight,
    adapter_up_weight,
    short_depthwise_filter,
    long_group_filter,
    skip_direct_scale,
    document_lengths,
    window_row_position,
):
    rows, chans = tokens.shape
    parts = frozen.shape[1]
    rank_dim = adapter_down_weight.shape[0]
    taps = short_depthwise_filter.shape[0]
    groups = long_group_filter.shape[0]
    shards = lax.axis_size("ctx")
    columns = lax.axis_size("tp")
    cap = 2 * rows // shards
    slots = shards * cap
    frozen = frozen.transpose(1, 0, 2)
    up = adapter_up_weight.transpose(1, 0, 2)
    pos_row = window_row_position.reshape(1, rows)
    vmem, far = pl.BlockSpec(memory_space=pltpu.VMEM), pl.BlockSpec(memory_space=pltpu.HBM)
    send, sel = pl.pallas_call(
        send_kernel,
        out_shape=(
            jax.ShapeDtypeStruct((shards, cap, parts * chans), BF),
            jax.ShapeDtypeStruct((slots, rows), BF),
        ),
        in_specs=[vmem, far],
        out_specs=(far, vmem),
        scratch_shapes=[
            pltpu.VMEM((parts, rows, chans), BF),
            pltpu.VMEM((parts, shards, cap, chans), BF),
            pltpu.SemaphoreType.DMA((parts,)),
            pltpu.SemaphoreType.DMA((parts,)),
        ],
        compiler_params=pltpu.CompilerParams(vmem_limit_bytes=66_000_000),
        cost_estimate=pl.CostEstimate(flops=1 << 30, bytes_accessed=5 << 20, transcendentals=0),
    )(pos_row, frozen)
    got = swap(send, "ctx")

    send, sel, document_lengths, short_depthwise_filter, adapter_down_weight = lax.optimization_barrier(
        (send, sel, document_lengths, short_depthwise_filter, adapter_down_weight)
    )
    (low_sum,) = whole(low_kernel, [((rank_dim, rows), F32)], flops=1 << 23, nbytes=1 << 19)(
        tokens, adapter_down_weight
    )
    for bit in range(3):
        low_sum = low_sum + partner(low_sum, "tp", 1 << bit)
    (send_low,) = whole(
        send_low_kernel, [((shards, cap, 128), BF)], flops=1 << 25, nbytes=1 << 19
    )(sel, pos_row, low_sum)
    (send_tok,) = whole(
        send_tokens_kernel, [((shards, cap, chans), BF)], flops=2 * slots * rows * chans, nbytes=2 << 20
    )(sel, tokens)
    first = lax.axis_index("ctx") * rows
    offsets = doc_offsets(first + jnp.arange(rows + 256, dtype=I32), document_lengths).astype(F32)
    off_row = offsets.reshape(1, rows + 256)
    tap_rows = short_depthwise_filter.reshape(taps * parts, chans).astype(F32)
    tap_rows = jnp.pad(tap_rows, ((0, 16 - taps * parts), (0, 0)))
    skip_row = skip_direct_scale.reshape(1, chans)
    blocks = rows // 128
    tall = 1024 * blocks + 128
    tiles = chans // 128
    fwd_bank, adj_bank = tiled(
        bank_kernel,
        tiles,
        [((8, 128), lambda i: (i, 0)), ((1, rows + 256), fixed2)],
        [((tiles, tall, 256), BF, (1, tall, 256), lambda i: (i, 0, 0))] * 2,
        [
            pltpu.VMEM((128 * blocks + 16, 256), BF),
            pltpu.VMEM((128 * blocks + 16, 256), BF),
            pltpu.VMEM((8, 128), F32),
            pltpu.VMEM((8, 128), F32),
        ],
        1 << 30,
        18 << 20,
        60_000_000,
    )(long_group_filter, off_row)
    got, send_low, send_tok, off_row, fwd_bank, adj_bank, tap_rows = lax.optimization_barrier(
        (got, send_low, send_tok, off_row, fwd_bank, adj_bank, tap_rows)
    )
    got_low = swap(send_low, "ctx")

    wide = 512
    steps = chans // wide
    pre, post, x, back, ahead, behind, place, low = tiled(
        post_kernel,
        steps,
        [((shards, cap, wide), lambda i, a=a: (0, 0, a * steps + i)) for a in range(parts)]
        + [
            ((shards, cap, 128), lambda i: (0, 0, 0)),
            ((parts, rank_dim, wide), at3),
            ((16, wide), at2),
            ((1, rows + 256), fixed2),
            ((rows, wide), at2),
        ],
        [
            ((parts, rows, chans), BF, (parts, rows, wide), at3),
            ((parts, rows, chans), BF, (parts, rows, wide), at3),
            ((rows, chans), BF, (rows, wide), at2),
            ((rows, chans), BF, (rows, wide), at2),
            ((144, chans), BF, (144, wide), at2),
            ((144, chans), BF, (144, wide), at2),
            ((rows, slots), BF, (rows, slots), fixed2),
            ((rank_dim, rows), BF, (rank_dim, rows), fixed2),
        ],
        [
            pltpu.VMEM((16, wide), F32),
            pltpu.VMEM((16, wide), F32),
            pltpu.VMEM((rows, rank_dim), BF),
            pltpu.VMEM((2, rows, 128), F32),
        ],
        1 << 30,
        8 << 20,
        60_000_000,
    )(got, got, got, got_low, up, tap_rows, off_row, cotangent)
    send_tok, ahead, behind = lax.optimization_barrier((send_tok, ahead, behind))
    from_prev = neighbour(ahead, 1)
    from_next = neighbour(behind, -1)
    got_tok = swap(send_tok, "ctx")
    mixer, sums, back_low_part = tiled(
        main_kernel,
        chans // 128,
        [
            ((parts, rows, 128), at3),
            ((parts, rows, 128), at3),
            ((rows, 128), at2),
            ((rows, 128), at2),
            ((144, 128), at2),
            ((144, 128), at2),
            ((rows, 128), at2),
            ((16, 128), at2),
            ((1, 128), at2),
            ((1, tall, 256), lambda i: (i, 0, 0)),
            ((1, tall, 256), lambda i: (i, 0, 0)),
            ((1, rows + 256), fixed2),
            ((rank_dim, rows), fixed2),
            ((parts, rank_dim, 128), at3),
        ],
        [
            ((rows, chans), BF, (rows, 128), at2),
            ((4, chans // 128, 24, 128), F32, (4, 1, 24, 128), lambda i: (0, i, 0, 0)),
            ((columns, rank_dim, rows), F32, (columns, rank_dim, rows), lambda i: (0, 0, 0)),
        ],
        [
            pltpu.VMEM((blocks, 128, 256), F32),
            pltpu.VMEM((2, rows + 128, 128), F32),
            pltpu.VMEM((1024, 128), BF),
            pltpu.VMEM((tall, 128), F32),
            pltpu.VMEM((tall, 128), F32),
            pltpu.VMEM((blocks, 1024, 256), F32),
            pltpu.VMEM((parts, rows, 128), F32),
            pltpu.VMEM((rank_dim, rows), F32),
        ],
        10 << 30,
        8 << 20,
        60_000_000,
    )(pre, post, x, back, from_prev, from_next, cotangent, tap_rows, skip_row, fwd_bank, adj_bank,
      off_row, low, up)
    got_tok, back_low_part = lax.optimization_barrier((got_tok, back_low_part))
    back_lows = swap(back_low_part, "tp")
    (pieces,) = whole(
        gather_kernel, [((shards, 24, 128), BF)], flops=1 << 26, nbytes=2 << 20
    )(back_lows, got_tok, place, sums)
    pieces = swap(pieces, "ctx")
    (pieces,) = whole(sum_kernel, [((shards, 24, 128), BF)], flops=1 << 20, nbytes=1 << 20)(pieces)
    pieces = swap(pieces, "ctx")
    grad_down, up_gradient, grad_short, grad_long, grad_skip = whole(
        spread_kernel,
        [
            ((rank_dim, chans), F32),
            ((parts, rank_dim, chans), F32),
            ((taps, parts, chans), F32),
            ((groups, 128), F32),
            ((chans // 128, 128), F32),
        ],
        flops=1 << 20,
        nbytes=1 << 20,
    )(pieces)
    return (
        mixer,
        grad_down,
        up_gradient.transpose(1, 0, 2),
        grad_short,
        grad_long,
        grad_skip.reshape(chans),
    )


def solution(mesh):
    placed = (
        P("ctx", "tp"),
        P("ctx", None, "tp"),
        P("ctx", "tp"),
        P(None, "tp"),
        P(None, None, "tp"),
        P(None, None, "tp"),
        P("tp", None),
        P("tp"),
        P(),
        P("ctx"),
    )
    return jax.shard_map(
        on_device,
        mesh=mesh,
        in_specs=placed,
        out_specs=(
            P("ctx", "tp"),
            P(None, "tp"),
            P(None, None, "tp"),
            P(None, None, "tp"),
            P("tp", None),
            P("tp"),
        ),
        check_vma=False,
    )
```
